32 devices in a mesh: gx: 8 (over z, core), gy: 4 (over y, x).
Axes of the slice: x: 2, y: 2, z: 4, core: 2. Of those that a mesh axis runs over, the one named last changes fastest.
Arguments:
- grad_pressure: float32 [64, 128, 1024], P('gx', 'gy'), may hold values from -6 to 6
- beta: float32 [3, 64, 128, 1024], P(None, 'gx', 'gy'), may hold values from 0.25 to 4
- tile_rows: int32 [8192], P(('gx', 'gy')), may hold values from 0 to 2047
- tile_owner: int32 [8192, 1], P(('gx', 'gy')), may hold values from 0 to 31; in each aligned block of 256 rows (0 to 255, 256 to 511, ...) at most 8 rows name the same one
- tile_slot: int32 [8192], P(('gx', 'gy')), may hold values from 0 to 255
- face_mask: int32 [8192, 128], P(('gx', 'gy')), may hold values 0 or 1
- heights: float32 [3, 8192, 128], P(None, ('gx', 'gy')), may hold values from -6 to 6
Outputs:
- grad_rhs: float32 [64, 128, 1024], P('gx', 'gy')
- grad_heights: float32 [3, 8192, 128], P(None, ('gx', 'gy'))
The draws below stay inside these ranges and needn't reach their ends.
Inputs may be any that keep to these rules, and one draw needn't show every extreme that they name: `tile_rows`: each entry indexes a row of 128 cells inside its own device's block. `tile_owner`: among the 256 tiles of one device no owner is named more than 8 times.
All inputs are finite; a program needn't handle non-finite values. No bound on the sum of `face_mask` on one device may be relied on, other than what follows from the above.
Results may differ from the reference program's by a relative error of at most 0.000025.
Values sent between devices are 32-bit elements; how exact they have to be, the bound alone decides.
A program may use at most 192 MiB of HBM per device.

```python
import math
import jax
import jax.numpy as jnp
import numpy as np

CX = 8
CY = 32
NZ = 1024
ITERS = 3
STEPS = 4
NT = 256
SLOTS = 256
CAP = 8
NX = 64
NY = 128
N_GX = 8
N_GY = 4


def place_ends(entries, own_key, low, top_value):
    spot = [jax.random.randint(jax.random.fold_in(own_key, axis), (), 0, length) for axis, length in enumerate(entries.shape)]
    main_axis = entries.shape.index(max(entries.shape))
    neighbour = spot[:main_axis] + [(spot[main_axis] + 1) % entries.shape[main_axis]] + spot[main_axis + 1:]
    return entries.at[tuple(spot)].set(low).at[tuple(neighbour)].set(top_value)


def levels(stream_key, dims, split, smallest, high):
    gain, own = 1.0, jax.random.fold_in(stream_key, 6)
    for axis_at, shards_of in split:
        draws = jnp.exp(jax.random.uniform(jax.random.fold_in(own, axis_at), (shards_of,), jnp.float32, smallest / len(split), high / len(split)))
        gain = gain * jnp.repeat(draws, dims[axis_at] // shards_of).reshape([-1 if axis == axis_at else 1 for axis in range(len(dims))])
    return gain


def deal_out(stream_key, own, number, rows, number_of, top, reach, lean):
    ranking = jax.random.permutation(stream_key, number_of)
    packed, usual = shares(number_of, rows * top, reach, lean, True), shares(number_of, rows * top, reach, lean, False)
    places = jnp.arange(number_of)

    def named(sizes, offset_by):
        used = int((sizes > 0).sum())
        fixed = max(1, used // 4)
        moved = fixed + (places - fixed + offset_by * (used - fixed)) % max(1, number_of - fixed)
        return jnp.zeros((number_of,), jnp.int32).at[ranking[jnp.where(places < fixed, places, moved)]].set(jnp.asarray(sizes, jnp.int32))

    sizes = jnp.where(number % 4 == 0, named(packed, number // 4), named(usual, number - number // 4 - 1))
    mixed = jax.random.permutation(jax.random.fold_in(own, 3), number_of)
    source_of, sink = mixed[0:number_of // 2 * 2:2], mixed[1:number_of // 2 * 2:2]
    slack = jnp.minimum(sizes[source_of] - 1, reach - sizes[sink]) // 2
    slack = jnp.where((source_of == ranking[0]) | (sink == ranking[0]) | (sizes[sink] == 0), 0, jnp.maximum(slack, 0))
    moved = jax.random.randint(jax.random.fold_in(own, 4), (number_of // 2,), 0, 1 << 20) % (slack + 1)
    sizes = sizes.at[source_of].add(-moved).at[sink].add(moved)
    items = jnp.searchsorted(jnp.cumsum(sizes), jnp.arange(rows * top), side="right").astype(jnp.int32)
    listing = items.reshape(top, rows).T
    listing = listing[jax.random.permutation(jax.random.fold_in(own, 1), rows)]
    offset_by = jax.random.randint(jax.random.fold_in(own, 2), (rows, 1), 0, top)
    return jnp.take_along_axis(listing, (jnp.arange(top)[None, :] + offset_by) % top, axis=1)


def shares(count, total, most, skew, full):
    weights = [(1 << 20) // math.isqrt(standing ** skew) + 1 for standing in range(1, count + 1)]
    largest = most if full else min(most, max(-(-total // count), total * weights[0] // sum(weights)))
    least = 1 if total - largest >= count - 1 else 0
    counts, surplus = [largest] + [least] * (count - 1), total - largest - least * (count - 1)
    while surplus > 0:
        movable = [i for i in range(1, count) if counts[i] < largest] or [i for i in range(1, count) if counts[i] < most]
        mass, budget = sum([weights[i] for i in movable]), surplus
        for i in movable:
            more = min(most - counts[i], max(1, budget * weights[i] // mass), surplus)
            counts[i] = counts[i] + more
            surplus = surplus - more
    return np.array(counts)


def scatter_about(key, extent, scale, reach, split=(), kind=jnp.bfloat16):
    result = jax.random.normal(key, extent, jnp.float32) * scale
    if len(split) > 0:
        result = levels(key, extent, split, -0.22, 0.18) * result
    return jnp.clip(result, min=-reach, max=reach).astype(kind)


def setup_inputs(seed: int = 0) -> dict:
    key_of = jax.random.split(jax.random.key(seed), 8)
    grad_pressure = scatter_about(key_of[0], (NX, NY, NZ), 1.0, 6.0, ((0, 8), (1, 4)), jnp.float32)
    beta = jnp.clip(jnp.exp(math.log(4.0) - 2.7725887 * jax.random.uniform(key_of[1], (3, NX, NY, NZ), jnp.float32) ** levels(key_of[1], (3, NX, NY, NZ), ((1, 8), (2, 4)), -0.2, 0.2)), 0.25, 4.0)
    tile_rows = place_ends(jax.random.randint(key_of[2], (N_GX * N_GY * NT,), 0, CX * CY * NZ // 128), jax.random.fold_in(key_of[2], 1), 0, (CX * CY * NZ // 128) - 1).astype(jnp.int32)
    tile_owner_keys = jax.random.split(jax.random.fold_in(key_of[3], 1), (N_GX * N_GY * NT) // NT)
    tile_owner_turns = jax.random.permutation(jax.random.fold_in(key_of[3], 3), (N_GX * N_GY * NT) // NT)
    tile_owner = jax.vmap(lambda own, number: deal_out(jax.random.fold_in(key_of[3], 2), own, number, NT, N_GX * N_GY, 1, CAP, 2))(tile_owner_keys, tile_owner_turns).reshape((N_GX * N_GY * NT, 1))
    tile_slot = place_ends(jax.random.randint(key_of[4], (N_GX * N_GY * NT,), 0, SLOTS), jax.random.fold_in(key_of[4], 1), 0, SLOTS - 1).astype(jnp.int32)
    face_mask = place_ends((jax.random.randint(key_of[5], (N_GX * N_GY * NT, 128), 0, 4) < 3).astype(jnp.int32), jax.random.fold_in(key_of[5], 1), 0, 1)
    heights = scatter_about(key_of[6], (3, N_GX * N_GY * SLOTS, 128), 1.0, 6.0, ((1, 32),), jnp.float32)
    return {"grad_pressure": grad_pressure, "beta": beta, "tile_rows": tile_rows, "tile_owner": tile_owner, "tile_slot": tile_slot, "face_mask": face_mask, "heights": heights}


LOW_BOUND = 0.1
HIGH_BOUND = 1.9


def omega_of(step_index):
    theta = 0.5 * (HIGH_BOUND + LOW_BOUND) + 0.5 * (HIGH_BOUND - LOW_BOUND) * math.cos(math.pi * (2 * step_index + 1) / (2 * STEPS))
    return 1.0 / theta


def shifted_low(field, axis_number):
    first = jnp.zeros_like(jnp.take(field, jnp.arange(1), axis=axis_number))
    rest = jnp.take(field, jnp.arange(field.shape[axis_number] - 1), axis=axis_number)
    return jnp.concatenate([first, rest], axis=axis_number)


def reference(grad_pressure, beta, tile_rows, tile_owner, tile_slot, face_mask, heights):
    beta_x, beta_y, beta_z = beta[0], beta[1], beta[2]
    low_x = shifted_low(beta_x, 0)
    low_y = shifted_low(beta_y, 1)
    low_z = shifted_low(beta_z, 2)
    diagonal = beta_x + low_x + beta_y + low_y + beta_z + low_z
    inv_diag = 1.0 / diagonal

    def operate(field):
        padded = jnp.pad(field, 1)
        inner = padded[1:-1, 1:-1, 1:-1]
        beside = beta_x * padded[2:, 1:-1, 1:-1] + low_x * padded[:-2, 1:-1, 1:-1]
        beside = beside + beta_y * padded[1:-1, 2:, 1:-1] + low_y * padded[1:-1, :-2, 1:-1]
        beside = beside + beta_z * padded[1:-1, 1:-1, 2:] + low_z * padded[1:-1, 1:-1, :-2]
        return diagonal * inner - beside

    adjoint = grad_pressure
    grad_rhs = jnp.zeros_like(grad_pressure)
    for cycle_index in range(ITERS):
        for step_index in reversed(range(STEPS)):
            scaled = omega_of(step_index) * inv_diag * adjoint
            grad_rhs = grad_rhs + scaled
            adjoint = adjoint - operate(scaled)

    peers = N_GX * N_GY
    blocks = NZ // 128
    device = jnp.arange(peers * NT, dtype=jnp.int32) // NT
    index_x = device // N_GY
    index_y = device % N_GY
    local_x = tile_rows // (CY * blocks)
    local_y = (tile_rows // blocks) % CY
    block_z = tile_rows % blocks
    grid_rows = grad_rhs.reshape(NX, NY, blocks, 128)
    picked = grid_rows[index_x * CX + local_x, index_y * CY + local_y, block_z]
    jump = face_mask.astype(jnp.float32) * picked
    global_slot = (tile_owner[:, 0] * SLOTS + tile_slot).astype(jnp.int32)
    table = jnp.zeros((peers * SLOTS, 128), jnp.float32).at[global_slot].add(jump)

    slope = 0.5 * (heights[2] - heights[0])
    bend = heights[2] - 2.0 * heights[1] + heights[0]
    denom = 1.0 + slope * slope
    factor = denom ** -1.5
    skew_term = -3.0 * slope * bend * denom ** -2.5
    grad_heights = jnp.stack([table * (factor - 0.5 * skew_term), -2.0 * table * factor, table * (factor + 0.5 * skew_term)])
    return grad_rhs, grad_heights
```

```python
import functools
import math

import jax
import jax.numpy as jnp
from jax import lax
from jax.experimental import pallas as pl
from jax.experimental.pallas import tpu as pltpu
from jax.sharding import PartitionSpec as P

ITERS = 3
STEPS = 4
CAP = 8
LANES = 128
ROWS = 8
WIDE = 256

LOW_BOUND = 0.1
HIGH_BOUND = 1.9

MESH = pl.DeviceIdType.MESH
EXACT = lax.Precision.HIGHEST


def omega_of(step_index):
    theta = 0.5 * (HIGH_BOUND + LOW_BOUND) + 0.5 * (HIGH_BOUND - LOW_BOUND) * math.cos(
        math.pi * (2 * step_index + 1) / (2 * STEPS)
    )
    return 1.0 / theta


def omega_at(step):
    j = STEPS - 1 - step % STEPS
    value = jnp.float32(omega_of(0))
    for index in range(1, STEPS):
        value = jnp.where(j == index, jnp.float32(omega_of(index)), value)
    return value


def picked_sum(selector, rows):
    high = rows.astype(jnp.bfloat16)
    rest = rows - high.astype(jnp.float32)
    middle = rest.astype(jnp.bfloat16)
    low = (rest - middle.astype(jnp.float32)).astype(jnp.bfloat16)
    parts = [jnp.dot(selector, part, preferred_element_type=jnp.float32) for part in (high, middle, low)]
    return parts[0] + (parts[1] + parts[2])


def kernel(
    n_x, n_y,
    grad_in, beta_in, rows_in, owner_in, slot_in, mask_in, heights_in,
    out_hbm, back_ref,
    grad_ref, beta_ref, rows_ref, owner_ref, slot_ref, mask_ref, heights_ref, load_sem,
    coeff, target, state, face_y, corner, halo_x, halo_y, halo_d,
    rim_x, rim_y, rim_face, face_coeff, edge_x, edge_y, near_x, near_y, line_x, line_y,
    flat, picked, place, send_rows, recv_rows, send_slots, recv_slots,
    rim_send, rim_recv, x_send, x_recv, y_send, y_recv, d_send, d_recv,
    edge_send, edge_recv, side_send, side_recv, row_send, row_recv, slot_send, slot_recv,
):
    X, Y, Z = grad_ref.shape
    groups = Y // ROWS
    blocks = Z // LANES
    chunks = Z // WIDE
    tiles = rows_ref.shape[0]
    peers = n_x * n_y
    slots = heights_ref.shape[1]
    ix = lax.axis_index("gx")
    iy = lax.axis_index("gy")
    me = ix * n_y + iy
    has_x = (ix > 0, ix < n_x - 1)
    has_y = (iy > 0, iy < n_y - 1)
    at_x = ((ix - 1, iy), (ix + 1, iy))
    at_y = ((ix, iy - 1), (ix, iy + 1))
    sides = (0, 1)
    total = ITERS * STEPS
    rounds = (total - 2) // 2

    for ref in (rim_x, rim_y, halo_x, halo_y, halo_d, edge_x, edge_y, line_x, line_y):
        ref[...] = jnp.zeros_like(ref)

    def peer_at(step):
        peer = (me + step) % peers
        return peer, (peer // n_y, peer % n_y)

    barrier = pltpu.get_barrier_semaphore()

    @pl.loop(1, peers)
    def _(step):
        pl.semaphore_signal(barrier, inc=1, device_id=peer_at(step)[1], device_id_type=MESH)

    names = ("owner", "slot", "beta", "grad", "rows", "mask", "heights")
    pairs = (
        (owner_in, owner_ref), (slot_in, slot_ref), (beta_in, beta_ref), (grad_in, grad_ref),
        (rows_in, rows_ref), (mask_in, mask_ref), (heights_in, heights_ref),
    )
    loads = {
        name: pltpu.make_async_copy(source, held, load_sem.at[index])
        for index, (name, (source, held)) in enumerate(zip(names, pairs))
    }
    for name in names:
        loads[name].start()
    for name in ("owner", "slot"):
        loads[name].wait()

    owner = owner_ref[...]
    peer_ids = lax.broadcasted_iota(jnp.int32, (peers, tiles), 0)
    named = (owner == peer_ids).astype(jnp.float32)
    down = lax.broadcasted_iota(jnp.int32, (tiles, tiles), 0)
    across = lax.broadcasted_iota(jnp.int32, (tiles, tiles), 1)
    earlier = (down < across).astype(jnp.bfloat16)
    counts = jnp.dot(named.astype(jnp.bfloat16), earlier, preferred_element_type=jnp.float32)
    position = jnp.sum(counts * named, axis=0, keepdims=True)
    spot = owner.astype(jnp.float32) * CAP + position
    spots = lax.broadcasted_iota(jnp.int32, (peers * CAP, tiles), 0).astype(jnp.float32)
    place[...] = (spot == spots).astype(jnp.float32).astype(jnp.bfloat16)
    spread = lax.broadcasted_iota(jnp.int32, (LANES, tiles), 0).astype(jnp.float32)
    spread = (spread == position).astype(jnp.float32)
    slot_rows = lax.dot_general(
        named * slot_ref[...].astype(jnp.float32), spread, (((1,), (1,)), ((), ())),
        preferred_element_type=jnp.float32, precision=EXACT,
    )
    send_slots[...] = slot_rows.reshape(peers, 1, LANES)

    loads["beta"].wait()
    for x in range(X):
        rim_face[x : x + 1, :] = beta_ref[1, x, Y - 1 : Y, :]

    pl.semaphore_wait(barrier, peers - 1)

    def remote(source, landing, send, recv, place_of):
        return pltpu.make_async_remote_copy(source, landing, send, recv, device_id=place_of, device_id_type=MESH)

    def rim_copies():
        return (
            (has_x, remote(beta_ref.at[0, X - 1], rim_x, rim_send.at[0], rim_recv.at[0], at_x[1])),
            (has_y, remote(rim_face, rim_y, rim_send.at[1], rim_recv.at[1], at_y[1])),
        )

    for has, copy in rim_copies():
        @pl.when(has[1])
        def _():
            copy.start()

    def slot_copy(step):
        peer, place_of = peer_at(step)
        return pltpu.make_async_remote_copy(
            send_slots.at[peer], recv_slots.at[me], slot_send.at[peer], slot_recv.at[me],
            device_id=place_of, device_id_type=MESH)

    def row_copy(step):
        peer, place_of = peer_at(step)
        return pltpu.make_async_remote_copy(
            send_rows.at[peer], recv_rows.at[me], row_send.at[peer], row_recv.at[me],
            device_id=place_of, device_id_type=MESH)

    def lanes(q):
        return pl.ds(q * WIDE, WIDE)

    def x_copy(par, kind, side, q, land):
        return remote(
            state.at[kind, (X - 1) * side, :, lanes(q)], halo_x.at[par, kind, land, :, lanes(q)],
            x_send.at[kind, side, q], x_recv.at[par, kind, land, q], at_x[side])

    def y_copy(par, kind, side, q, land):
        return remote(
            face_y.at[kind, side, :, lanes(q)], halo_y.at[par, kind, land, :, lanes(q)],
            y_send.at[kind, side, q], y_recv.at[par, kind, land, q], at_y[side])

    def d_copy(par, dx, dy, q, land):
        return remote(
            corner.at[dx, dy, :, lanes(q)], halo_d.at[par, land[0], land[1], :, lanes(q)],
            d_send.at[dx, dy, q], d_recv.at[par, land[0], land[1], q], (at_x[dx][0], at_y[dy][1]))

    def copies_of(par, kind, q, arriving):
        found = []
        for side in sides:
            land = side if arriving else 1 - side
            found.append((has_x[side], x_copy(par, kind, side, q, land)))
        for side in sides:
            land = side if arriving else 1 - side
            found.append((has_y[side], y_copy(par, kind, side, q, land)))
        if kind == 0:
            for dx in sides:
                for dy in sides:
                    land = (dx, dy) if arriving else (1 - dx, 1 - dy)
                    found.append((jnp.logical_and(has_x[dx], has_y[dy]), d_copy(par, dx, dy, q, land)))
        return found

    def start_sends(par, kind, q, go=None):
        for has, copy in copies_of(par, kind, q, False):
            @pl.when(has if go is None else jnp.logical_and(has, go))
            def _():
                copy.start()

    def wait_sends(kind, q):
        for has, copy in copies_of(0, kind, q, False):
            @pl.when(has)
            def _():
                copy.wait_send()

    def wait_arrivals(par, kind, q):
        for has, copy in copies_of(par, kind, q, True):
            @pl.when(has)
            def _():
                copy.wait_recv()

    def edge_copy(side, q, land):
        return remote(
            coeff.at[1 - side, (X - 1) * side, :, lanes(q)], edge_x.at[land, :, lanes(q)],
            edge_send.at[side, q], edge_recv.at[land, q], at_x[side])

    def side_copies(side, land):
        return (
            (has_y[side], remote(face_coeff.at[side], edge_y.at[land], side_send.at[0, side], side_recv.at[0, land], at_y[side])),
            (has_x[side], remote(near_x.at[side], line_x.at[land], side_send.at[1, side], side_recv.at[1, land], at_x[side])),
            (has_y[side], remote(near_y.at[side], line_y.at[land], side_send.at[2, side], side_recv.at[2, land], at_y[side])),
        )

    def row_index(width):
        return lax.broadcasted_iota(jnp.int32, (ROWS, width), 0)

    z_ids = lax.broadcasted_iota(jnp.int32, (ROWS, Z), 1)

    def from_below(tile, row):
        return jnp.where(row_index(tile.shape[1]) == 0, row, pltpu.roll(tile, 1, 0))

    def from_above(tile, row):
        return jnp.where(row_index(tile.shape[1]) == ROWS - 1, row, pltpu.roll(tile, ROWS - 1, 0))

    first = omega_of(STEPS - 1)

    def keep_faces(kind, value, x, g, cut):
        if g == 0:
            face_y[kind, 0, x : x + 1, cut] = value[:1, :]
        if g == groups - 1:
            face_y[kind, 1, x : x + 1, cut] = value[ROWS - 1 :, :]
        if kind == 0 and x in (0, X - 1):
            if g == 0:
                corner[0 if x == 0 else 1, 0, :, cut] = value[:1, :]
            if g == groups - 1:
                corner[0 if x == 0 else 1, 1, :, cut] = value[ROWS - 1 :, :]

    def prepare(x, g):
        r = slice(g * ROWS, (g + 1) * ROWS)
        up_x, up_y, up_z = beta_ref[0, x, r, :], beta_ref[1, x, r, :], beta_ref[2, x, r, :]
        low_x = rim_x[r, :] if x == 0 else beta_ref[0, x - 1, r, :]
        row = rim_y[x : x + 1, :] if g == 0 else beta_ref[1, x, g * ROWS - 1 : g * ROWS, :]
        low_y = from_below(up_y, row)
        low_z = jnp.where(z_ids == 0, 0.0, pltpu.roll(up_z, 1, 1))
        inv = 1.0 / (up_x + low_x + up_y + low_y + up_z + low_z)
        up_z = jnp.where(z_ids == Z - 1, 0.0, up_z)
        for index, value in enumerate((up_x, low_x, up_y, low_y, up_z, low_z)):
            value = value * inv
            coeff[index, x, r, :] = value
            if index == 3 and g == 0:
                face_coeff[0, x : x + 1, :] = value[:1, :]
                if x in (0, X - 1):
                    near_x[0 if x == 0 else 1, 0] = value[:1, :]
            if index == 2 and g == groups - 1:
                face_coeff[1, x : x + 1, :] = value[ROWS - 1 :, :]
                if x in (0, X - 1):
                    near_x[0 if x == 0 else 1, 1] = value[ROWS - 1 :, :]
            if (index, x) in ((1, 0), (0, X - 1)):
                if g == 0:
                    near_y[0, 1 - index] = value[:1, :]
                if g == groups - 1:
                    near_y[1, 1 - index] = value[ROWS - 1 :, :]
        value = inv * grad_ref[x, r, :]
        target[x, r, :] = value
        value = first * value
        state[0, x, r, :] = value
        keep_faces(0, value, x, g, slice(0, Z))

    def update(kind, omega, x, g, q, par=None):
        source = 1 - kind
        r = slice(g * ROWS, (g + 1) * ROWS)
        cut = slice(q * WIDE, (q + 1) * WIDE)
        start, stop = max(q * WIDE - LANES, 0), min((q + 1) * WIDE + LANES, Z)
        inner = slice(q * WIDE - start, q * WIDE - start + WIDE)
        wide = state[source, x, r, start:stop]
        s = wide[:, inner]
        if g < groups - 1:
            above_row = state[source, x, (g + 1) * ROWS : (g + 1) * ROWS + 1, cut]
        else:
            above_row = 0.0 if par is None else halo_y[par, 1, 1, x : x + 1, cut]
        if g > 0:
            below_row = state[source, x, g * ROWS - 1 : g * ROWS, cut]
        else:
            below_row = 0.0 if par is None else halo_y[par, 1, 0, x : x + 1, cut]
        beside = target[x, r, cut] - s
        beside += coeff[2, x, r, cut] * from_above(s, above_row)
        beside += coeff[3, x, r, cut] * from_below(s, below_row)
        beside += coeff[4, x, r, cut] * pltpu.roll(wide, stop - start - 1, 1)[:, inner]
        beside += coeff[5, x, r, cut] * pltpu.roll(wide, 1, 1)[:, inner]
        if x < X - 1:
            beside += coeff[0, x, r, cut] * state[source, x + 1, r, cut]
        elif par is not None:
            beside += coeff[0, x, r, cut] * halo_x[par, 1, 1, r, cut]
        if x > 0:
            beside += coeff[1, x, r, cut] * state[source, x - 1, r, cut]
        elif par is not None:
            beside += coeff[1, x, r, cut] * halo_x[par, 1, 0, r, cut]
        value = s + omega * beside
        state[kind, x, r, cut] = value
        keep_faces(kind, value, x, g, cut)

    def update_all(kind, omega, q, par=None):
        for x in range(X):
            for g in range(groups):
                update(kind, omega, x, g, q, par)

    def complete_own(par, omega, q):
        cut = slice(q * WIDE, (q + 1) * WIDE)
        for side in sides:
            x = (X - 1) * side
            for g in range(groups):
                r = slice(g * ROWS, (g + 1) * ROWS)
                state[1, x, r, cut] += omega * (coeff[1 - side, x, r, cut] * halo_x[par, 0, side, r, cut])
        for side in sides:
            more = omega * (face_coeff[side, :, cut] * halo_y[par, 0, side, :, cut])
            row = (Y - 1) * side
            for x in range(X):
                state[1, x, row : row + 1, cut] += more[x : x + 1, :]

    def complete_halo(par, omega, q):
        cut = slice(q * WIDE, (q + 1) * WIDE)
        for side in sides:
            x = (X - 1) * side
            for g in range(groups):
                r = slice(g * ROWS, (g + 1) * ROWS)
                halo_x[par, 1, side, r, cut] += omega * (edge_x[side, r, cut] * state[0, x, r, cut])
            for dy in sides:
                row = (Y - 1) * dy
                halo_x[par, 1, side, row : row + 1, cut] += omega * (
                    line_x[side, dy, :, cut] * halo_d[par, side, dy, :, cut])
        for side in sides:
            halo_y[par, 1, side, :, cut] += omega * (edge_y[side, :, cut] * face_y[0, side, :, cut])
            for dx in sides:
                x = (X - 1) * dx
                halo_y[par, 1, side, x : x + 1, cut] += omega * (
                    line_y[side, dx, :, cut] * halo_d[par, dx, side, :, cut])

    loads["grad"].wait()
    for x in range(1, X):
        for g in range(1, groups):
            prepare(x, g)
    (_, rim_x_copy), (_, rim_y_copy) = rim_copies()

    @pl.when(has_x[0])
    def _():
        rim_x_copy.wait_recv()

    for g in range(1, groups):
        prepare(0, g)

    @pl.when(has_y[0])
    def _():
        rim_y_copy.wait_recv()

    for x in range(X):
        prepare(x, 0)

    for q in range(chunks):
        start_sends(0, 0, q)
    for side in sides:
        for has, copy in side_copies(side, 1 - side):
            @pl.when(has)
            def _():
                copy.start()

    for q in range(chunks):
        update_all(1, omega_of(STEPS - 1 - 1 % STEPS), q)
        start_sends(0, 1, q)
        for side in sides:
            @pl.when(has_x[side])
            def _():
                edge_copy(side, q, 1 - side).start()

    for has, copy in rim_copies():
        @pl.when(has[1])
        def _():
            copy.wait_send()

    @pl.loop(1, peers)
    def _(step):
        slot_copy(step).start()

    recv_slots[me] = send_slots[me]

    for side in sides:
        for has, copy in side_copies(side, side):
            @pl.when(has)
            def _():
                copy.wait_recv()

    def round_body(number, carry):
        par = number % 2
        more = number < rounds - 1
        omega = omega_at(2 * number + 1)
        omega_even = omega_at(2 * number + 2)
        omega_odd = omega_at(2 * number + 3)

        def own(q):
            wait_arrivals(par, 0, q)
            wait_sends(1, q)
            complete_own(par, omega, q)

        def odd(q):
            update_all(1, omega_odd, q)
            start_sends(1 - par, 1, q, more)

        own(0)
        for q in range(chunks):
            if q + 1 < chunks:
                own(q + 1)
            wait_arrivals(par, 1, q)
            for side in sides:
                @pl.when(jnp.logical_and(has_x[side], number == 0))
                def _():
                    edge_copy(side, q, side).wait_recv()
            complete_halo(par, omega, q)
            wait_sends(0, q)
            update_all(0, omega_even, q, par)
            start_sends(1 - par, 0, q)
            if q > 0:
                odd(q - 1)
        odd(chunks - 1)
        return carry

    lax.fori_loop(0, rounds, round_body, 0)
    for q in range(chunks):
        wait_arrivals(rounds % 2, 0, q)
        complete_own(rounds % 2, omega_of(STEPS - 1 - (total - 1) % STEPS), q)
    store = pltpu.make_async_copy(state.at[1], out_hbm, load_sem.at[7])
    store.start()
    for q in range(chunks):
        wait_sends(0, q)
    for side in sides:
        for q in range(chunks):
            @pl.when(has_x[side])
            def _():
                edge_copy(side, q, 1 - side).wait_send()
        for has, copy in side_copies(side, 1 - side):
            @pl.when(has)
            def _():
                copy.wait_send()
    for name in ("rows", "mask", "heights"):
        loads[name].wait()

    for x in range(X):
        for b in range(blocks):
            start = (x * blocks + b) * Y
            flat[start : start + Y, :] = state[1, x, :, b * LANES : (b + 1) * LANES]

    unroll = 8

    @pl.loop(0, tiles // unroll)
    def _(chunk):
        for lane in range(unroll):
            t = chunk * unroll + lane
            row = rows_ref[t]
            line = lax.div(row, blocks)
            x = lax.div(line, Y)
            at = (x * blocks + row - line * blocks) * Y + line - x * Y
            picked[pl.ds(t, 1), :] = flat[pl.ds(at, 1), :]

    jumps = picked[...] * mask_ref[...].astype(jnp.float32)
    send_rows[...] = picked_sum(place[...], jumps).reshape(peers, CAP, LANES)

    @pl.loop(1, peers)
    def _(step):
        row_copy(step).start()

    recv_rows[me] = send_rows[me]

    @pl.loop(1, peers)
    def _(step):
        peer, place_of = peer_at(step)
        pltpu.make_async_remote_copy(
            send_slots.at[peer], recv_slots.at[peer], slot_send.at[peer], slot_recv.at[peer],
            device_id=place_of, device_id_type=MESH).wait()

    own = lax.broadcasted_iota(jnp.int32, (peers, CAP, LANES), 1)
    lane_ids = lax.broadcasted_iota(jnp.int32, (peers, CAP, LANES), 2)
    got = jnp.broadcast_to(recv_slots[...], (peers, CAP, LANES))
    slot_of = jnp.sum(jnp.where(own == lane_ids, got, 0.0), axis=2, keepdims=True)
    slot_of = slot_of.reshape(peers * CAP, 1)
    slot_ids = lax.broadcasted_iota(jnp.int32, (peers * CAP, slots), 1).astype(jnp.float32)
    chosen = (slot_of == slot_ids).astype(jnp.float32).T.astype(jnp.bfloat16)

    slope = 0.5 * (heights_ref[2] - heights_ref[0])
    bend = heights_ref[2] - 2.0 * heights_ref[1] + heights_ref[0]
    denom = 1.0 + slope * slope
    factor = 1.0 / (denom * jnp.sqrt(denom))
    skew = -3.0 * slope * bend * factor / denom

    @pl.loop(1, peers)
    def _(step):
        peer, place_of = peer_at(step)
        pltpu.make_async_remote_copy(
            send_rows.at[peer], recv_rows.at[peer], row_send.at[peer], row_recv.at[peer],
            device_id=place_of, device_id_type=MESH).wait()

    table = picked_sum(chosen, recv_rows[...].reshape(peers * CAP, LANES))
    back_ref[0] = table * (factor - 0.5 * skew)
    back_ref[1] = -2.0 * table * factor
    back_ref[2] = table * (factor + 0.5 * skew)
    store.wait()


def shards(grad_pressure, beta, tile_rows, tile_owner, tile_slot, face_mask, heights):
    n_x, n_y = lax.axis_size("gx"), lax.axis_size("gy")
    peers = n_x * n_y
    X, Y, Z = grad_pressure.shape
    chunks = Z // WIDE
    tiles = tile_rows.shape[0]
    f32 = jnp.float32
    vmem = pl.BlockSpec(memory_space=pltpu.VMEM)
    hbm = pl.BlockSpec(memory_space=pltpu.HBM)
    dma = pltpu.SemaphoreType.DMA
    return pl.pallas_call(
        functools.partial(kernel, n_x, n_y),
        out_shape=(
            jax.ShapeDtypeStruct((X, Y, Z), f32),
            jax.ShapeDtypeStruct(heights.shape, f32),
        ),
        in_specs=[hbm] * 7,
        out_specs=(hbm, vmem),
        scratch_shapes=[
            pltpu.VMEM((X, Y, Z), f32),
            pltpu.VMEM(beta.shape, f32),
            pltpu.SMEM((tiles,), jnp.int32),
            pltpu.VMEM((1, tiles), jnp.int32),
            pltpu.VMEM((1, tiles), jnp.int32),
            pltpu.VMEM(face_mask.shape, jnp.int32),
            pltpu.VMEM(heights.shape, f32),
            dma((8,)),
            pltpu.VMEM((6, X, Y, Z), f32),
            pltpu.VMEM((X, Y, Z), f32),
            pltpu.VMEM((2, X, Y, Z), f32),
            pltpu.VMEM((2, 2, X, Z), f32),
            pltpu.VMEM((2, 2, 1, Z), f32),
            pltpu.VMEM((2, 2, 2, Y, Z), f32),
            pltpu.VMEM((2, 2, 2, X, Z), f32),
            pltpu.VMEM((2, 2, 2, 1, Z), f32),
            pltpu.VMEM((Y, Z), f32),
            pltpu.VMEM((X, Z), f32),
            pltpu.VMEM((X, Z), f32),
            pltpu.VMEM((2, X, Z), f32),
            pltpu.VMEM((2, Y, Z), f32),
            pltpu.VMEM((2, X, Z), f32),
            pltpu.VMEM((2, 2, 1, Z), f32),
            pltpu.VMEM((2, 2, 1, Z), f32),
            pltpu.VMEM((2, 2, 1, Z), f32),
            pltpu.VMEM((2, 2, 1, Z), f32),
            pltpu.VMEM((X * Y * Z // LANES, LANES), f32),
            pltpu.VMEM((tiles, LANES), f32),
            pltpu.VMEM((peers * CAP, tiles), jnp.bfloat16),
            pltpu.VMEM((peers, CAP, LANES), f32),
            pltpu.VMEM((peers, CAP, LANES), f32),
            pltpu.VMEM((peers, 1, LANES), f32),
            pltpu.VMEM((peers, 1, LANES), f32),
            dma((2,)),
            dma((2,)),
            dma((2, 2, chunks)),
            dma((2, 2, 2, chunks)),
            dma((2, 2, chunks)),
            dma((2, 2, 2, chunks)),
            dma((2, 2, chunks)),
            dma((2, 2, 2, chunks)),
            dma((2, chunks)),
            dma((2, chunks)),
            dma((3, 2)),
            dma((3, 2)),
            dma((peers,)),
            dma((peers,)),
            dma((peers,)),
            dma((peers,)),
        ],
        compiler_params=pltpu.CompilerParams(
            collective_id=0, has_side_effects=True, vmem_limit_bytes=56 * 1024 * 1024
        ),
    )(grad_pressure, beta, tile_rows, tile_owner.reshape(1, -1), tile_slot.reshape(1, -1), face_mask, heights)


def solution(mesh):
    in_specs = (
        P("gx", "gy", None),
        P(None, "gx", "gy", None),
        P(("gx", "gy")),
        P(("gx", "gy"), None),
        P(("gx", "gy")),
        P(("gx", "gy"), None),
        P(None, ("gx", "gy"), None),
    )
    out_specs = (P("gx", "gy", None), P(None, ("gx", "gy"), None))
    return jax.shard_map(shards, mesh=mesh, in_specs=in_specs, out_specs=out_specs, check_vma=False)
```

```python
import functools
import math

import jax
import jax.numpy as jnp
from jax import lax
from jax.experimental import pallas as pl
from jax.experimental.pallas import tpu as pltpu
from jax.sharding import PartitionSpec as P

ITERS = 3
STEPS = 4
CAP = 8
LANES = 128
ROWS = 8
UNROLL = 16
WIDE = 256

LOW_BOUND = 0.1
HIGH_BOUND = 1.9

MESH = pl.DeviceIdType.MESH
EXACT = lax.Precision.HIGHEST


def omega_of(step_index):
    theta = 0.5 * (HIGH_BOUND + LOW_BOUND) + 0.5 * (HIGH_BOUND - LOW_BOUND) * math.cos(
        math.pi * (2 * step_index + 1) / (2 * STEPS)
    )
    return 1.0 / theta


def omega_at(step):
    j = STEPS - 1 - step % STEPS
    value = jnp.float32(omega_of(0))
    for index in range(1, STEPS):
        value = jnp.where(j == index, jnp.float32(omega_of(index)), value)
    return value


def picked_sum(selector, rows):
    high = rows.astype(jnp.bfloat16)
    rest = rows - high.astype(jnp.float32)
    middle = rest.astype(jnp.bfloat16)
    low = (rest - middle.astype(jnp.float32)).astype(jnp.bfloat16)
    parts = [jnp.dot(selector, part, preferred_element_type=jnp.float32) for part in (high, middle, low)]
    return parts[0] + (parts[1] + parts[2])


def kernel(
    n_x, n_y,
    grad_in, beta_in, rows_in, owner_in, slot_in, mask_in, heights_in,
    out_ref, back_ref,
    grad_ref, beta_ref, rows_ref, owner_ref, slot_ref, mask_ref, heights_ref, load_sem,
    coeff, target, state, face_y, corner, halo_x, halo_y, halo_d,
    rim_x, rim_y, rim_face, face_coeff, edge_x, edge_y, near_x, near_y, line_x, line_y,
    flat, picked, spots_ref, chosen, scales, place, send_rows, recv_rows, send_slots, recv_slots,
    rim_send, rim_recv, x_send, x_recv, y_send, y_recv, d_send, d_recv,
    edge_send, edge_recv, side_send, side_recv, row_send, row_recv, slot_send, slot_recv,
):
    X, Y, Z = grad_ref.shape
    groups = Y // ROWS
    blocks = Z // LANES
    chunks = Z // WIDE
    tiles = rows_ref.shape[0]
    peers = n_x * n_y
    slots = heights_ref.shape[1]
    ix = lax.axis_index("gx")
    iy = lax.axis_index("gy")
    me = ix * n_y + iy
    has_x = (ix > 0, ix < n_x - 1)
    has_y = (iy > 0, iy < n_y - 1)
    at_x = ((ix - 1, iy), (ix + 1, iy))
    at_y = ((ix, iy - 1), (ix, iy + 1))
    sides = (0, 1)
    total = ITERS * STEPS
    rounds = (total - 2) // 2

    for ref in (rim_x, rim_y, halo_x, halo_y, halo_d, edge_x, edge_y, line_x, line_y):
        ref[...] = jnp.zeros_like(ref)

    def peer_at(step):
        peer = (me + step) % peers
        return peer, (peer // n_y, peer % n_y)

    barrier = pltpu.get_barrier_semaphore()

    @pl.loop(1, peers)
    def _(step):
        pl.semaphore_signal(barrier, inc=1, device_id=peer_at(step)[1], device_id_type=MESH)

    names = ("owner", "slot", "beta", "grad", "rows", "mask", "heights")
    pairs = (
        (owner_in, owner_ref), (slot_in, slot_ref), (beta_in, beta_ref), (grad_in, grad_ref),
        (rows_in, rows_ref), (mask_in, mask_ref), (heights_in, heights_ref),
    )
    loads = {
        name: pltpu.make_async_copy(source, held, load_sem.at[index])
        for index, (name, (source, held)) in enumerate(zip(names, pairs))
    }
    for name in names:
        loads[name].start()
    for name in ("owner", "slot"):
        loads[name].wait()

    owner = owner_ref[...]
    peer_ids = lax.broadcasted_iota(jnp.int32, (peers, tiles), 0)
    named = (owner == peer_ids).astype(jnp.float32)
    down = lax.broadcasted_iota(jnp.int32, (tiles, tiles), 0)
    across = lax.broadcasted_iota(jnp.int32, (tiles, tiles), 1)
    earlier = (down < across).astype(jnp.bfloat16)
    counts = jnp.dot(named.astype(jnp.bfloat16), earlier, preferred_element_type=jnp.float32)
    position = jnp.sum(counts * named, axis=0, keepdims=True)
    spot = owner.astype(jnp.float32) * CAP + position
    spots = lax.broadcasted_iota(jnp.int32, (peers * CAP, tiles), 0).astype(jnp.float32)
    place[...] = (spot == spots).astype(jnp.float32).astype(jnp.bfloat16)
    spread = lax.broadcasted_iota(jnp.int32, (LANES, tiles), 0).astype(jnp.float32)
    spread = (spread == position).astype(jnp.float32)
    slot_rows = lax.dot_general(
        named * slot_ref[...].astype(jnp.float32), spread, (((1,), (1,)), ((), ())),
        preferred_element_type=jnp.float32, precision=EXACT,
    )
    send_slots[...] = slot_rows.reshape(peers, 1, LANES)

    loads["beta"].wait()
    for x in range(X):
        rim_face[x : x + 1, :] = beta_ref[1, x, Y - 1 : Y, :]

    pl.semaphore_wait(barrier, peers - 1)

    def remote(source, landing, send, recv, place_of):
        return pltpu.make_async_remote_copy(source, landing, send, recv, device_id=place_of, device_id_type=MESH)

    def rim_copies():
        return (
            (has_x, remote(beta_ref.at[0, X - 1], rim_x, rim_send.at[0], rim_recv.at[0], at_x[1])),
            (has_y, remote(rim_face, rim_y, rim_send.at[1], rim_recv.at[1], at_y[1])),
        )

    for has, copy in rim_copies():
        @pl.when(has[1])
        def _():
            copy.start()

    def slot_copy(step):
        peer, place_of = peer_at(step)
        return pltpu.make_async_remote_copy(
            send_slots.at[peer], recv_slots.at[me], slot_send.at[peer], slot_recv.at[me],
            device_id=place_of, device_id_type=MESH)

    def row_copy(step):
        peer, place_of = peer_at(step)
        return pltpu.make_async_remote_copy(
            send_rows.at[peer], recv_rows.at[me], row_send.at[peer], row_recv.at[me],
            device_id=place_of, device_id_type=MESH)

    def lanes(q):
        return pl.ds(q * WIDE, WIDE)

    def x_copy(par, kind, side, q, land):
        return remote(
            state.at[kind, (X - 1) * side, :, lanes(q)], halo_x.at[par, kind, land, :, lanes(q)],
            x_send.at[kind, side, q], x_recv.at[par, kind, land, q], at_x[side])

    def y_copy(par, kind, side, q, land):
        return remote(
            face_y.at[kind, side, :, lanes(q)], halo_y.at[par, kind, land, :, lanes(q)],
            y_send.at[kind, side, q], y_recv.at[par, kind, land, q], at_y[side])

    def d_copy(par, dx, dy, q, land):
        return remote(
            corner.at[dx, dy, :, lanes(q)], halo_d.at[par, land[0], land[1], :, lanes(q)],
            d_send.at[dx, dy, q], d_recv.at[par, land[0], land[1], q], (at_x[dx][0], at_y[dy][1]))

    def copies_of(par, kind, q, arriving):
        found = []
        for side in sides:
            land = side if arriving else 1 - side
            found.append((has_x[side], x_copy(par, kind, side, q, land)))
        for side in sides:
            land = side if arriving else 1 - side
            found.append((has_y[side], y_copy(par, kind, side, q, land)))
        if kind == 0:
            for dx in sides:
                for dy in sides:
                    land = (dx, dy) if arriving else (1 - dx, 1 - dy)
                    found.append((jnp.logical_and(has_x[dx], has_y[dy]), d_copy(par, dx, dy, q, land)))
        return found

    def start_sends(par, kind, q, go=None):
        for has, copy in copies_of(par, kind, q, False):
            @pl.when(has if go is None else jnp.logical_and(has, go))
            def _():
                copy.start()

    def wait_sends(kind, q):
        for has, copy in copies_of(0, kind, q, False):
            @pl.when(has)
            def _():
                copy.wait_send()

    def wait_arrivals(par, kind, q):
        for has, copy in copies_of(par, kind, q, True):
            @pl.when(has)
            def _():
                copy.wait_recv()

    def edge_copy(side, q, land):
        return remote(
            coeff.at[1 - side, (X - 1) * side, :, lanes(q)], edge_x.at[land, :, lanes(q)],
            edge_send.at[side, q], edge_recv.at[land, q], at_x[side])

    def side_copies(side, land):
        return (
            (has_y[side], remote(face_coeff.at[side], edge_y.at[land], side_send.at[0, side], side_recv.at[0, land], at_y[side])),
            (has_x[side], remote(near_x.at[side], line_x.at[land], side_send.at[1, side], side_recv.at[1, land], at_x[side])),
            (has_y[side], remote(near_y.at[side], line_y.at[land], side_send.at[2, side], side_recv.at[2, land], at_y[side])),
        )

    def row_index(width):
        return lax.broadcasted_iota(jnp.int32, (ROWS, width), 0)

    z_ids = lax.broadcasted_iota(jnp.int32, (ROWS, Z), 1)

    def from_below(tile, row):
        return jnp.where(row_index(tile.shape[1]) == 0, row, pltpu.roll(tile, 1, 0))

    def from_above(tile, row):
        return jnp.where(row_index(tile.shape[1]) == ROWS - 1, row, pltpu.roll(tile, ROWS - 1, 0))

    first = omega_of(STEPS - 1)

    def keep_faces(kind, value, x, g, cut):
        if g == 0:
            face_y[kind, 0, x : x + 1, cut] = value[:1, :]
        if g == groups - 1:
            face_y[kind, 1, x : x + 1, cut] = value[ROWS - 1 :, :]
        if kind == 0 and x in (0, X - 1):
            if g == 0:
                corner[0 if x == 0 else 1, 0, :, cut] = value[:1, :]
            if g == groups - 1:
                corner[0 if x == 0 else 1, 1, :, cut] = value[ROWS - 1 :, :]

    def prepare(x, g):
        r = slice(g * ROWS, (g + 1) * ROWS)
        up_x, up_y, up_z = beta_ref[0, x, r, :], beta_ref[1, x, r, :], beta_ref[2, x, r, :]
        low_x = rim_x[r, :] if x == 0 else beta_ref[0, x - 1, r, :]
        row = rim_y[x : x + 1, :] if g == 0 else beta_ref[1, x, g * ROWS - 1 : g * ROWS, :]
        low_y = from_below(up_y, row)
        low_z = jnp.where(z_ids == 0, 0.0, pltpu.roll(up_z, 1, 1))
        inv = 1.0 / (up_x + low_x + up_y + low_y + up_z + low_z)
        up_z = jnp.where(z_ids == Z - 1, 0.0, up_z)
        for index, value in enumerate((up_x, low_x, up_y, low_y, up_z, low_z)):
            value = value * inv
            coeff[index, x, r, :] = value
            if index == 3 and g == 0:
                face_coeff[0, x : x + 1, :] = value[:1, :]
                if x in (0, X - 1):
                    near_x[0 if x == 0 else 1, 0] = value[:1, :]
            if index == 2 and g == groups - 1:
                face_coeff[1, x : x + 1, :] = value[ROWS - 1 :, :]
                if x in (0, X - 1):
                    near_x[0 if x == 0 else 1, 1] = value[ROWS - 1 :, :]
            if (index, x) in ((1, 0), (0, X - 1)):
                if g == 0:
                    near_y[0, 1 - index] = value[:1, :]
                if g == groups - 1:
                    near_y[1, 1 - index] = value[ROWS - 1 :, :]
        value = inv * grad_ref[x, r, :]
        target[x, r, :] = value
        value = first * value
        state[0, x, r, :] = value
        keep_faces(0, value, x, g, slice(0, Z))

    def update(kind, omega, x, g, q, par=None):
        source = 1 - kind
        r = slice(g * ROWS, (g + 1) * ROWS)
        cut = slice(q * WIDE, (q + 1) * WIDE)
        start, stop = max(q * WIDE - LANES, 0), min((q + 1) * WIDE + LANES, Z)
        inner = slice(q * WIDE - start, q * WIDE - start + WIDE)
        wide = state[source, x, r, start:stop]
        s = wide[:, inner]
        if g < groups - 1:
            above_row = state[source, x, (g + 1) * ROWS : (g + 1) * ROWS + 1, cut]
        else:
            above_row = 0.0 if par is None else halo_y[par, 1, 1, x : x + 1, cut]
        if g > 0:
            below_row = state[source, x, g * ROWS - 1 : g * ROWS, cut]
        else:
            below_row = 0.0 if par is None else halo_y[par, 1, 0, x : x + 1, cut]
        beside = target[x, r, cut] - s
        beside += coeff[2, x, r, cut] * from_above(s, above_row)
        beside += coeff[3, x, r, cut] * from_below(s, below_row)
        beside += coeff[4, x, r, cut] * pltpu.roll(wide, stop - start - 1, 1)[:, inner]
        beside += coeff[5, x, r, cut] * pltpu.roll(wide, 1, 1)[:, inner]
        if x < X - 1:
            beside += coeff[0, x, r, cut] * state[source, x + 1, r, cut]
        elif par is not None:
            beside += coeff[0, x, r, cut] * halo_x[par, 1, 1, r, cut]
        if x > 0:
            beside += coeff[1, x, r, cut] * state[source, x - 1, r, cut]
        elif par is not None:
            beside += coeff[1, x, r, cut] * halo_x[par, 1, 0, r, cut]
        value = s + omega * beside
        state[kind, x, r, cut] = value
        keep_faces(kind, value, x, g, cut)

    def update_all(kind, omega, q, par=None):
        for x in range(X):
            for g in range(groups):
                update(kind, omega, x, g, q, par)

    def complete_own(par, omega, q):
        cut = slice(q * WIDE, (q + 1) * WIDE)
        for side in sides:
            x = (X - 1) * side
            for g in range(groups):
                r = slice(g * ROWS, (g + 1) * ROWS)
                state[1, x, r, cut] += omega * (coeff[1 - side, x, r, cut] * halo_x[par, 0, side, r, cut])
        for side in sides:
            more = omega * (face_coeff[side, :, cut] * halo_y[par, 0, side, :, cut])
            row = (Y - 1) * side
            for x in range(X):
                state[1, x, row : row + 1, cut] += more[x : x + 1, :]

    def complete_halo(par, omega, q):
        cut = slice(q * WIDE, (q + 1) * WIDE)
        for side in sides:
            x = (X - 1) * side
            for g in range(groups):
                r = slice(g * ROWS, (g + 1) * ROWS)
                halo_x[par, 1, side, r, cut] += omega * (edge_x[side, r, cut] * state[0, x, r, cut])
            for dy in sides:
                row = (Y - 1) * dy
                halo_x[par, 1, side, row : row + 1, cut] += omega * (
                    line_x[side, dy, :, cut] * halo_d[par, side, dy, :, cut])
        for side in sides:
            halo_y[par, 1, side, :, cut] += omega * (edge_y[side, :, cut] * face_y[0, side, :, cut])
            for dx in sides:
                x = (X - 1) * dx
                halo_y[par, 1, side, x : x + 1, cut] += omega * (
                    line_y[side, dx, :, cut] * halo_d[par, dx, side, :, cut])

    loads["grad"].wait()
    for x in range(1, X):
        for g in range(1, groups):
            prepare(x, g)
    (_, rim_x_copy), (_, rim_y_copy) = rim_copies()

    @pl.when(has_x[0])
    def _():
        rim_x_copy.wait_recv()

    for g in range(1, groups):
        prepare(0, g)

    @pl.when(has_y[0])
    def _():
        rim_y_copy.wait_recv()

    for x in range(X):
        prepare(x, 0)

    for q in range(chunks):
        start_sends(0, 0, q)
    for side in sides:
        for has, copy in side_copies(side, 1 - side):
            @pl.when(has)
            def _():
                copy.start()

    for q in range(chunks):
        update_all(1, omega_of(STEPS - 1 - 1 % STEPS), q)
        start_sends(0, 1, q)
        for side in sides:
            @pl.when(has_x[side])
            def _():
                edge_copy(side, q, 1 - side).start()

    for has, copy in rim_copies():
        @pl.when(has[1])
        def _():
            copy.wait_send()

    @pl.loop(1, peers)
    def _(step):
        slot_copy(step).start()

    recv_slots[me] = send_slots[me]

    for side in sides:
        for has, copy in side_copies(side, side):
            @pl.when(has)
            def _():
                copy.wait_recv()

    def round_body(number, carry):
        par = number % 2
        more = number < rounds - 1
        omega = omega_at(2 * number + 1)
        omega_even = omega_at(2 * number + 2)
        omega_odd = omega_at(2 * number + 3)

        def own(q):
            wait_arrivals(par, 0, q)
            wait_sends(1, q)
            complete_own(par, omega, q)

        def odd(q):
            update_all(1, omega_odd, q)
            start_sends(1 - par, 1, q, more)

        own(0)
        for q in range(chunks):
            if q + 1 < chunks:
                own(q + 1)
            wait_arrivals(par, 1, q)
            for side in sides:
                @pl.when(jnp.logical_and(has_x[side], number == 0))
                def _():
                    edge_copy(side, q, side).wait_recv()
            complete_halo(par, omega, q)
            wait_sends(0, q)
            update_all(0, omega_even, q, par)
            start_sends(1 - par, 0, q)
            if q > 0:
                odd(q - 1)
        odd(chunks - 1)
        return carry

    lax.fori_loop(0, rounds, round_body, 0)
    for name in ("rows", "mask", "heights"):
        loads[name].wait()

    @pl.loop(0, tiles // UNROLL)
    def _(part):
        for lane in range(UNROLL):
            t = part * UNROLL + lane
            row = rows_ref[t]
            line = lax.div(row, blocks)
            x = lax.div(line, Y)
            spots_ref[t] = (x * blocks + row - line * blocks) * Y + line - x * Y

    @pl.loop(1, peers)
    def _(step):
        peer, place_of = peer_at(step)
        pltpu.make_async_remote_copy(
            send_slots.at[peer], recv_slots.at[peer], slot_send.at[peer], slot_recv.at[peer],
            device_id=place_of, device_id_type=MESH).wait()

    own = lax.broadcasted_iota(jnp.int32, (peers, CAP, LANES), 1)
    lane_ids = lax.broadcasted_iota(jnp.int32, (peers, CAP, LANES), 2)
    got = jnp.broadcast_to(recv_slots[...], (peers, CAP, LANES))
    slot_of = jnp.sum(jnp.where(own == lane_ids, got, 0.0), axis=2, keepdims=True)
    slot_of = slot_of.reshape(peers * CAP, 1)
    slot_ids = lax.broadcasted_iota(jnp.int32, (peers * CAP, slots), 1).astype(jnp.float32)
    chosen[...] = (slot_of == slot_ids).astype(jnp.float32).T.astype(jnp.bfloat16)

    slope = 0.5 * (heights_ref[2] - heights_ref[0])
    bend = heights_ref[2] - 2.0 * heights_ref[1] + heights_ref[0]
    denom = 1.0 + slope * slope
    factor = 1.0 / (denom * jnp.sqrt(denom))
    skew = -3.0 * slope * bend * factor / denom
    scales[0] = factor - 0.5 * skew
    scales[1] = -2.0 * factor
    scales[2] = factor + 0.5 * skew

    for q in range(chunks):
        wait_arrivals(rounds % 2, 0, q)
        complete_own(rounds % 2, omega_of(STEPS - 1 - (total - 1) % STEPS), q)
    for q in range(chunks):
        wait_sends(0, q)
    for side in sides:
        for q in range(chunks):
            @pl.when(has_x[side])
            def _():
                edge_copy(side, q, 1 - side).wait_send()
        for has, copy in side_copies(side, 1 - side):
            @pl.when(has)
            def _():
                copy.wait_send()
    for x in range(X):
        for b in range(blocks):
            start = (x * blocks + b) * Y
            value = state[1, x, :, b * LANES : (b + 1) * LANES]
            flat[start : start + Y, :] = value
            out_ref[x, :, b * LANES : (b + 1) * LANES] = value

    @pl.loop(0, tiles // UNROLL)
    def _(part):
        for lane in range(UNROLL):
            t = part * UNROLL + lane
            picked[pl.ds(t, 1), :] = flat[pl.ds(spots_ref[t], 1), :]

    jumps = picked[...] * mask_ref[...].astype(jnp.float32)
    send_rows[...] = picked_sum(place[...], jumps).reshape(peers, CAP, LANES)

    @pl.loop(1, peers)
    def _(step):
        row_copy(step).start()

    recv_rows[me] = send_rows[me]

    @pl.loop(1, peers)
    def _(step):
        peer, place_of = peer_at(step)
        pltpu.make_async_remote_copy(
            send_rows.at[peer], recv_rows.at[peer], row_send.at[peer], row_recv.at[peer],
            device_id=place_of, device_id_type=MESH).wait()

    table = picked_sum(chosen[...], recv_rows[...].reshape(peers * CAP, LANES))
    for index in range(3):
        back_ref[index] = table * scales[index]


def hand_over(first_held, second_held, first_out, second_out, sem):
    stores = []
    for held, landing in ((first_held, first_out), (second_held, second_out)):
        for index in range(held.shape[0]):
            stores.append(pltpu.make_async_copy(held.at[index], landing.at[index], sem.at[len(stores)]))
    for store in stores:
        store.start()
    for store in stores:
        store.wait()


def shards(grad_pressure, beta, tile_rows, tile_owner, tile_slot, face_mask, heights):
    n_x, n_y = lax.axis_size("gx"), lax.axis_size("gy")
    peers = n_x * n_y
    X, Y, Z = grad_pressure.shape
    chunks = Z // WIDE
    tiles = tile_rows.shape[0]
    f32 = jnp.float32
    vmem = pl.BlockSpec(memory_space=pltpu.VMEM)
    hbm = pl.BlockSpec(memory_space=pltpu.HBM)
    dma = pltpu.SemaphoreType.DMA
    results = pl.pallas_call(
        functools.partial(kernel, n_x, n_y),
        out_shape=(pltpu.VMEM((X, Y, Z), f32), pltpu.VMEM(heights.shape, f32)),
        in_specs=[hbm] * 7,
        out_specs=(vmem, vmem),
        scratch_shapes=[
            pltpu.VMEM((X, Y, Z), f32),
            pltpu.VMEM(beta.shape, f32),
            pltpu.SMEM((tiles,), jnp.int32),
            pltpu.VMEM((1, tiles), jnp.int32),
            pltpu.VMEM((1, tiles), jnp.int32),
            pltpu.VMEM(face_mask.shape, jnp.int32),
            pltpu.VMEM(heights.shape, f32),
            dma((8,)),
            pltpu.VMEM((6, X, Y, Z), f32),
            pltpu.VMEM((X, Y, Z), f32),
            pltpu.VMEM((2, X, Y, Z), f32),
            pltpu.VMEM((2, 2, X, Z), f32),
            pltpu.VMEM((2, 2, 1, Z), f32),
            pltpu.VMEM((2, 2, 2, Y, Z), f32),
            pltpu.VMEM((2, 2, 2, X, Z), f32),
            pltpu.VMEM((2, 2, 2, 1, Z), f32),
            pltpu.VMEM((Y, Z), f32),
            pltpu.VMEM((X, Z), f32),
            pltpu.VMEM((X, Z), f32),
            pltpu.VMEM((2, X, Z), f32),
            pltpu.VMEM((2, Y, Z), f32),
            pltpu.VMEM((2, X, Z), f32),
            pltpu.VMEM((2, 2, 1, Z), f32),
            pltpu.VMEM((2, 2, 1, Z), f32),
            pltpu.VMEM((2, 2, 1, Z), f32),
            pltpu.VMEM((2, 2, 1, Z), f32),
            pltpu.VMEM((X * Y * Z // LANES, LANES), f32),
            pltpu.VMEM((tiles, LANES), f32),
            pltpu.SMEM((tiles,), jnp.int32),
            pltpu.VMEM((heights.shape[1], peers * CAP), jnp.bfloat16),
            pltpu.VMEM(heights.shape, f32),
            pltpu.VMEM((peers * CAP, tiles), jnp.bfloat16),
            pltpu.VMEM((peers, CAP, LANES), f32),
            pltpu.VMEM((peers, CAP, LANES), f32),
            pltpu.VMEM((peers, 1, LANES), f32),
            pltpu.VMEM((peers, 1, LANES), f32),
            dma((2,)),
            dma((2,)),
            dma((2, 2, chunks)),
            dma((2, 2, 2, chunks)),
            dma((2, 2, chunks)),
            dma((2, 2, 2, chunks)),
            dma((2, 2, chunks)),
            dma((2, 2, 2, chunks)),
            dma((2, chunks)),
            dma((2, chunks)),
            dma((3, 2)),
            dma((3, 2)),
            dma((peers,)),
            dma((peers,)),
            dma((peers,)),
            dma((peers,)),
        ],
        compiler_params=pltpu.CompilerParams(
            collective_id=0, has_side_effects=True, vmem_limit_bytes=60 * 1024 * 1024
        ),
    )(grad_pressure, beta, tile_rows, tile_owner.reshape(1, -1), tile_slot.reshape(1, -1), face_mask, heights)
    parts = sum(result.shape[0] for result in results)
    return pl.pallas_call(
        hand_over,
        out_shape=tuple(jax.ShapeDtypeStruct(result.shape, f32) for result in results),
        in_specs=[vmem] * 2,
        out_specs=(hbm, hbm),
        scratch_shapes=[dma((parts,))],
    )(*[pltpu.with_memory_space_constraint(result, pltpu.VMEM) for result in results])


def solution(mesh):
    in_specs = (
        P("gx", "gy", None),
        P(None, "gx", "gy", None),
        P(("gx", "gy")),
        P(("gx", "gy"), None),
        P(("gx", "gy")),
        P(("gx", "gy"), None),
        P(None, ("gx", "gy"), None),
    )
    out_specs = (P("gx", "gy", None), P(None, ("gx", "gy"), None))
    return jax.shard_map(shards, mesh=mesh, in_specs=in_specs, out_specs=out_specs, check_vma=False)
```

```python
import functools
import math

import jax
import jax.numpy as jnp
from jax import lax
from jax.experimental import pallas as pl
from jax.experimental.pallas import tpu as pltpu
from jax.sharding import PartitionSpec as P

ITERS = 3
STEPS = 4
CAP = 8
LANES = 128
ROWS = 8
UNROLL = 16
WIDE = 256

LOW_BOUND = 0.1
HIGH_BOUND = 1.9

MESH = pl.DeviceIdType.MESH
EXACT = lax.Precision.HIGHEST


def omega_of(step_index):
    theta = 0.5 * (HIGH_BOUND + LOW_BOUND) + 0.5 * (HIGH_BOUND - LOW_BOUND) * math.cos(
        math.pi * (2 * step_index + 1) / (2 * STEPS)
    )
    return 1.0 / theta


def omega_at(step):
    j = STEPS - 1 - step % STEPS
    value = jnp.float32(omega_of(0))
    for index in range(1, STEPS):
        value = jnp.where(j == index, jnp.float32(omega_of(index)), value)
    return value


def picked_sum(selector, rows):
    high = rows.astype(jnp.bfloat16)
    rest = rows - high.astype(jnp.float32)
    middle = rest.astype(jnp.bfloat16)
    low = (rest - middle.astype(jnp.float32)).astype(jnp.bfloat16)
    parts = [jnp.dot(selector, part, preferred_element_type=jnp.float32) for part in (high, middle, low)]
    return parts[0] + (parts[1] + parts[2])


def kernel(
    n_x, n_y,
    grad_in, beta_in, rows_in, owner_in, slot_in, mask_in, heights_in,
    out_ref, back_ref,
    grad_ref, beta_ref, rows_ref, owner_ref, slot_ref, mask_ref, heights_ref, load_sem,
    coeff, target, state, face_y, corner, halo_x, halo_y, halo_d,
    rim_x, rim_y, rim_face, face_coeff, edge_x, edge_y, line_x, line_y,
    part_x, part_y, grad_y, near_x, near_y, near_d, raw_x, raw_y, raw_by, raw_bx, raw_d,
    flat, picked, spots_ref, chosen, scales, place, send_rows, recv_rows, send_slots, recv_slots,
    x_send, x_recv, y_send, y_recv, d_send, d_recv,
    raw_send, raw_recv, lone_send, lone_recv, row_send, row_recv, slot_send, slot_recv,
):
    X, Y, Z = grad_ref.shape
    groups = Y // ROWS
    blocks = Z // LANES
    chunks = Z // WIDE
    tiles = rows_ref.shape[0]
    peers = n_x * n_y
    slots = heights_ref.shape[1]
    ix = lax.axis_index("gx")
    iy = lax.axis_index("gy")
    me = ix * n_y + iy
    has_x = (ix > 0, ix < n_x - 1)
    has_y = (iy > 0, iy < n_y - 1)
    at_x = ((ix - 1, iy), (ix + 1, iy))
    at_y = ((ix, iy - 1), (ix, iy + 1))
    sides = (0, 1)
    total = ITERS * STEPS
    rounds = (total - 2) // 2

    for ref in (rim_x, rim_y, halo_x, halo_y, halo_d, edge_x, edge_y, line_x, line_y, raw_d):
        ref[...] = jnp.zeros_like(ref)

    def peer_at(step):
        peer = (me + step) % peers
        return peer, (peer // n_y, peer % n_y)

    barrier = pltpu.get_barrier_semaphore()

    @pl.loop(1, peers)
    def _(step):
        pl.semaphore_signal(barrier, inc=1, device_id=peer_at(step)[1], device_id_type=MESH)

    names = ("owner", "slot", "beta", "grad", "rows", "mask", "heights")
    pairs = (
        (owner_in, owner_ref), (slot_in, slot_ref), (beta_in, beta_ref), (grad_in, grad_ref),
        (rows_in, rows_ref), (mask_in, mask_ref), (heights_in, heights_ref),
    )
    loads = {
        name: pltpu.make_async_copy(source, held, load_sem.at[index])
        for index, (name, (source, held)) in enumerate(zip(names, pairs))
    }
    for name in names:
        loads[name].start()
    for name in ("owner", "slot"):
        loads[name].wait()

    owner = owner_ref[...]
    peer_ids = lax.broadcasted_iota(jnp.int32, (peers, tiles), 0)
    named = (owner == peer_ids).astype(jnp.float32)
    down = lax.broadcasted_iota(jnp.int32, (tiles, tiles), 0)
    across = lax.broadcasted_iota(jnp.int32, (tiles, tiles), 1)
    earlier = (down < across).astype(jnp.bfloat16)
    counts = jnp.dot(named.astype(jnp.bfloat16), earlier, preferred_element_type=jnp.float32)
    position = jnp.sum(counts * named, axis=0, keepdims=True)
    spot = owner.astype(jnp.float32) * CAP + position
    spots = lax.broadcasted_iota(jnp.int32, (peers * CAP, tiles), 0).astype(jnp.float32)
    place[...] = (spot == spots).astype(jnp.float32).astype(jnp.bfloat16)
    spread = lax.broadcasted_iota(jnp.int32, (LANES, tiles), 0).astype(jnp.float32)
    spread = (spread == position).astype(jnp.float32)
    slot_rows = lax.dot_general(
        named * slot_ref[...].astype(jnp.float32), spread, (((1,), (1,)), ((), ())),
        preferred_element_type=jnp.float32, precision=EXACT,
    )
    send_slots[...] = slot_rows.reshape(peers, 1, LANES)

    z_ids = lax.broadcasted_iota(jnp.int32, (ROWS, Z), 1)

    def row_index(width):
        return lax.broadcasted_iota(jnp.int32, (ROWS, width), 0)

    def from_below(tile, row):
        return jnp.where(row_index(tile.shape[1]) == 0, row, pltpu.roll(tile, 1, 0))

    def from_above(tile, row):
        return jnp.where(row_index(tile.shape[1]) == ROWS - 1, row, pltpu.roll(tile, ROWS - 1, 0))

    def part_of_diagonal(x, g):
        r = slice(g * ROWS, (g + 1) * ROWS)
        up_y, up_z = beta_ref[1, x, r, :], beta_ref[2, x, r, :]
        low_y = from_below(up_y, 0.0 if g == 0 else beta_ref[1, x, g * ROWS - 1 : g * ROWS, :])
        value = beta_ref[0, x, r, :] + up_y + low_y + up_z + jnp.where(z_ids == 0, 0.0, pltpu.roll(up_z, 1, 1))
        return value if x == 0 else value + beta_ref[0, x - 1, r, :]

    loads["beta"].wait()
    for x in range(X):
        rim_face[x : x + 1, :] = beta_ref[1, x, Y - 1 : Y, :]
        for g in range(groups):
            if x in (0, X - 1) or g in (0, groups - 1):
                value = part_of_diagonal(x, g)
                if x in (0, X - 1):
                    part_x[0 if x == 0 else 1, g * ROWS : (g + 1) * ROWS, :] = value
                if g == 0:
                    part_y[0, x : x + 1, :] = value[:1, :]
                if g == groups - 1:
                    part_y[1, x : x + 1, :] = value[ROWS - 1 :, :]
    for side in sides:
        near_x[side] = beta_ref[1, (X - 1) * side, Y - 1 : Y, :]
        near_y[side] = beta_ref[0, X - 1, (Y - 1) * side : (Y - 1) * side + 1, :]
        for dy in sides:
            near_d[side, dy, 0] = beta_ref[0, X - 1, (Y - 1) * dy : (Y - 1) * dy + 1, :]
            near_d[side, dy, 1] = beta_ref[1, (X - 1) * side, Y - 1 : Y, :]
    loads["grad"].wait()
    for x in range(X):
        for side in sides:
            grad_y[side, x : x + 1, :] = grad_ref[x, (Y - 1) * side : (Y - 1) * side + 1, :]

    pl.semaphore_wait(barrier, peers - 1)

    def remote(source, landing, send, recv, place_of):
        return pltpu.make_async_remote_copy(source, landing, send, recv, device_id=place_of, device_id_type=MESH)

    def slot_copy(step):
        peer, place_of = peer_at(step)
        return pltpu.make_async_remote_copy(
            send_slots.at[peer], recv_slots.at[me], slot_send.at[peer], slot_recv.at[me],
            device_id=place_of, device_id_type=MESH)

    def row_copy(step):
        peer, place_of = peer_at(step)
        return pltpu.make_async_remote_copy(
            send_rows.at[peer], recv_rows.at[me], row_send.at[peer], row_recv.at[me],
            device_id=place_of, device_id_type=MESH)

    def lanes(q):
        return pl.ds(q * WIDE, WIDE)

    def x_copy(par, kind, side, q, land):
        return remote(
            state.at[kind, (X - 1) * side, :, lanes(q)], halo_x.at[par, kind, land, :, lanes(q)],
            x_send.at[kind, side, q], x_recv.at[par, kind, land, q], at_x[side])

    def y_copy(par, kind, side, q, land):
        return remote(
            face_y.at[kind, side, :, lanes(q)], halo_y.at[par, kind, land, :, lanes(q)],
            y_send.at[kind, side, q], y_recv.at[par, kind, land, q], at_y[side])

    def d_copy(par, dx, dy, q, land):
        return remote(
            corner.at[dx, dy, :, lanes(q)], halo_d.at[par, land[0], land[1], :, lanes(q)],
            d_send.at[dx, dy, q], d_recv.at[par, land[0], land[1], q], (at_x[dx][0], at_y[dy][1]))

    def copies_of(par, kind, q, arriving):
        found = []
        for side in sides:
            land = side if arriving else 1 - side
            found.append((has_x[side], x_copy(par, kind, side, q, land)))
        for side in sides:
            land = side if arriving else 1 - side
            found.append((has_y[side], y_copy(par, kind, side, q, land)))
        if kind == 0:
            for dx in sides:
                for dy in sides:
                    land = (dx, dy) if arriving else (1 - dx, 1 - dy)
                    found.append((jnp.logical_and(has_x[dx], has_y[dy]), d_copy(par, dx, dy, q, land)))
        return found

    def start_sends(par, kind, q, go=None):
        for has, copy in copies_of(par, kind, q, False):
            @pl.when(has if go is None else jnp.logical_and(has, go))
            def _():
                copy.start()

    def wait_sends(kind, q):
        for has, copy in copies_of(0, kind, q, False):
            @pl.when(has)
            def _():
                copy.wait_send()

    def wait_arrivals(par, kind, q):
        for has, copy in copies_of(par, kind, q, True):
            @pl.when(has)
            def _():
                copy.wait_recv()

    def lone_copies(side, arriving):
        land = side if arriving else 1 - side
        found = [
            (has_x[side], remote(near_x.at[side], raw_by.at[land], lone_send.at[0, side], lone_recv.at[0, land], at_x[side])),
            (has_y[side], remote(near_y.at[side], raw_bx.at[land], lone_send.at[1, side], lone_recv.at[1, land], at_y[side])),
        ]
        for dy in sides:
            other = dy if arriving else 1 - dy
            found.append((jnp.logical_and(has_x[side], has_y[dy]), remote(
                near_d.at[side, dy], raw_d.at[land, other], lone_send.at[2 + dy, side], lone_recv.at[2 + other, land],
                (at_x[side][0], at_y[dy][1]))))
        return found

    def raw_copies(q, arriving):
        cut = lanes(q)
        found = []
        for side in sides:
            land = side if arriving else 1 - side
            sources = (
                (has_x, at_x, 0, beta_ref.at[0, X - 1, :, cut], rim_x.at[:, cut]),
                (has_y, at_y, 1, rim_face.at[:, cut], rim_y.at[:, cut]),
                (has_x, at_x, 2, grad_ref.at[(X - 1) * side, :, cut], raw_x.at[0, land, :, cut]),
                (has_y, at_y, 3, grad_y.at[side, :, cut], raw_y.at[0, land, :, cut]),
                (has_x, at_x, 4, part_x.at[side, :, cut], raw_x.at[1, land, :, cut]),
                (has_y, at_y, 5, part_y.at[side, :, cut], raw_y.at[1, land, :, cut]),
            )
            for has, at, kind, source, landing in sources:
                if kind > 1 or side == (0 if arriving else 1):
                    found.append((has[side], remote(
                        source, landing, raw_send.at[kind, side, q], raw_recv.at[kind, land, q], at[side])))
        return found

    first = omega_of(STEPS - 1)

    def keep_faces(kind, value, x, g, cut):
        if g == 0:
            face_y[kind, 0, x : x + 1, cut] = value[:1, :]
        if g == groups - 1:
            face_y[kind, 1, x : x + 1, cut] = value[ROWS - 1 :, :]
        if kind == 0 and x in (0, X - 1):
            if g == 0:
                corner[0 if x == 0 else 1, 0, :, cut] = value[:1, :]
            if g == groups - 1:
                corner[0 if x == 0 else 1, 1, :, cut] = value[ROWS - 1 :, :]

    def prepare(x, g, q=None):
        r = slice(g * ROWS, (g + 1) * ROWS)
        start, stop = (0, Z) if q is None else (q * WIDE, (q + 1) * WIDE)
        cut = slice(start, stop)
        wide = slice(max(start - LANES, 0), stop)
        inner = slice(start - wide.start, stop - wide.start)
        z_at = z_ids[:, cut]
        up_x, up_y, up_z = beta_ref[0, x, r, cut], beta_ref[1, x, r, cut], beta_ref[2, x, r, wide]
        low_x = rim_x[r, cut] if x == 0 else beta_ref[0, x - 1, r, cut]
        row = rim_y[x : x + 1, cut] if g == 0 else beta_ref[1, x, g * ROWS - 1 : g * ROWS, cut]
        low_y = from_below(up_y, row)
        low_z = jnp.where(z_at == 0, 0.0, pltpu.roll(up_z, 1, 1)[:, inner])
        up_z = up_z[:, inner]
        inv = 1.0 / (up_x + low_x + up_y + low_y + up_z + low_z)
        up_z = jnp.where(z_at == Z - 1, 0.0, up_z)
        for index, value in enumerate((up_x, low_x, up_y, low_y, up_z, low_z)):
            value = value * inv
            coeff[index, x, r, cut] = value
            if index == 3 and g == 0:
                face_coeff[0, x : x + 1, cut] = value[:1, :]
            if index == 2 and g == groups - 1:
                face_coeff[1, x : x + 1, cut] = value[ROWS - 1 :, :]
        value = inv * grad_ref[x, r, cut]
        target[x, r, cut] = value
        state[1, x, r, cut] = first * value

    def prepare_halo_x(side, q):
        cut = slice(q * WIDE, (q + 1) * WIDE)
        for g in range(groups):
            r = slice(g * ROWS, (g + 1) * ROWS)
            shared = beta_ref[0, X - 1, r, cut] if side else rim_x[r, cut]
            total_of = raw_x[1, side, r, cut]
            if side:
                total_of += shared
            if g == 0:
                total_of += jnp.where(row_index(WIDE) == 0, raw_d[side, 0, 1, :, cut], 0.0)
            inv = 1.0 / total_of
            halo_x[1, 1, side, r, cut] = first * (inv * raw_x[0, side, r, cut])
            edge_x[side, r, cut] = shared * inv
            if g == 0:
                line_x[side, 0, :, cut] = raw_d[side, 0, 1, :, cut] * inv[:1, :]
            if g == groups - 1:
                line_x[side, 1, :, cut] = raw_by[side, :, cut] * inv[ROWS - 1 :, :]

    def prepare_halo_y(side, q):
        cut = slice(q * WIDE, (q + 1) * WIDE)
        shared = rim_face[:, cut] if side else rim_y[:, cut]
        total_of = raw_y[1, side, :, cut]
        if side:
            total_of += shared
        planes = lax.broadcasted_iota(jnp.int32, (X, WIDE), 0)
        total_of += jnp.where(planes == 0, raw_d[0, side, 0, :, cut], 0.0)
        inv = 1.0 / total_of
        halo_y[1, 1, side, :, cut] = first * (inv * raw_y[0, side, :, cut])
        edge_y[side, :, cut] = shared * inv
        line_y[side, 0, :, cut] = raw_d[0, side, 0, :, cut] * inv[:1, :]
        line_y[side, 1, :, cut] = raw_bx[side, :, cut] * inv[X - 1 :, :]

    def update(kind, omega, x, g, q, par=None):
        source = 1 - kind
        r = slice(g * ROWS, (g + 1) * ROWS)
        cut = slice(q * WIDE, (q + 1) * WIDE)
        start, stop = max(q * WIDE - LANES, 0), min((q + 1) * WIDE + LANES, Z)
        inner = slice(q * WIDE - start, q * WIDE - start + WIDE)
        wide = state[source, x, r, start:stop]
        s = wide[:, inner]
        if g < groups - 1:
            above_row = state[source, x, (g + 1) * ROWS : (g + 1) * ROWS + 1, cut]
        else:
            above_row = 0.0 if par is None else halo_y[par, 1, 1, x : x + 1, cut]
        if g > 0:
            below_row = state[source, x, g * ROWS - 1 : g * ROWS, cut]
        else:
            below_row = 0.0 if par is None else halo_y[par, 1, 0, x : x + 1, cut]
        beside = target[x, r, cut] - s
        beside += coeff[2, x, r, cut] * from_above(s, above_row)
        beside += coeff[3, x, r, cut] * from_below(s, below_row)
        beside += coeff[4, x, r, cut] * pltpu.roll(wide, stop - start - 1, 1)[:, inner]
        beside += coeff[5, x, r, cut] * pltpu.roll(wide, 1, 1)[:, inner]
        if x < X - 1:
            beside += coeff[0, x, r, cut] * state[source, x + 1, r, cut]
        elif par is not None:
            beside += coeff[0, x, r, cut] * halo_x[par, 1, 1, r, cut]
        if x > 0:
            beside += coeff[1, x, r, cut] * state[source, x - 1, r, cut]
        elif par is not None:
            beside += coeff[1, x, r, cut] * halo_x[par, 1, 0, r, cut]
        value = s + omega * beside
        state[kind, x, r, cut] = value
        keep_faces(kind, value, x, g, cut)

    def update_all(kind, omega, q, par=None):
        for x in range(X):
            for g in range(groups):
                update(kind, omega, x, g, q, par)

    def complete_own(par, omega, q):
        cut = slice(q * WIDE, (q + 1) * WIDE)
        for side in sides:
            x = (X - 1) * side
            for g in range(groups):
                r = slice(g * ROWS, (g + 1) * ROWS)
                state[1, x, r, cut] += omega * (coeff[1 - side, x, r, cut] * halo_x[par, 0, side, r, cut])
        for side in sides:
            more = omega * (face_coeff[side, :, cut] * halo_y[par, 0, side, :, cut])
            row = (Y - 1) * side
            for x in range(X):
                state[1, x, row : row + 1, cut] += more[x : x + 1, :]

    def complete_halo(par, omega, q):
        cut = slice(q * WIDE, (q + 1) * WIDE)
        for side in sides:
            x = (X - 1) * side
            for g in range(groups):
                r = slice(g * ROWS, (g + 1) * ROWS)
                halo_x[par, 1, side, r, cut] += omega * (edge_x[side, r, cut] * state[0, x, r, cut])
            for dy in sides:
                row = (Y - 1) * dy
                halo_x[par, 1, side, row : row + 1, cut] += omega * (
                    line_x[side, dy, :, cut] * halo_d[par, side, dy, :, cut])
        for side in sides:
            halo_y[par, 1, side, :, cut] += omega * (edge_y[side, :, cut] * face_y[0, side, :, cut])
            for dx in sides:
                x = (X - 1) * dx
                halo_y[par, 1, side, x : x + 1, cut] += omega * (
                    line_y[side, dx, :, cut] * halo_d[par, dx, side, :, cut])

    for side in sides:
        for has, copy in lone_copies(side, False):
            @pl.when(has)
            def _():
                copy.start()
    for q in range(chunks):
        for has, copy in raw_copies(q, False):
            @pl.when(has)
            def _():
                copy.start()

    @pl.loop(1, peers)
    def _(step):
        slot_copy(step).start()

    recv_slots[me] = send_slots[me]
    for x in range(1, X):
        for g in range(1, groups):
            prepare(x, g)

    for name in ("rows", "mask", "heights"):
        loads[name].wait()

    @pl.loop(0, tiles // UNROLL)
    def _(part):
        for lane in range(UNROLL):
            t = part * UNROLL + lane
            row = rows_ref[t]
            line = lax.div(row, blocks)
            x = lax.div(line, Y)
            spots_ref[t] = (x * blocks + row - line * blocks) * Y + line - x * Y

    slope = 0.5 * (heights_ref[2] - heights_ref[0])
    bend = heights_ref[2] - 2.0 * heights_ref[1] + heights_ref[0]
    denom = 1.0 + slope * slope
    factor = 1.0 / (denom * jnp.sqrt(denom))
    skew = -3.0 * slope * bend * factor / denom
    scales[0] = factor - 0.5 * skew
    scales[1] = -2.0 * factor
    scales[2] = factor + 0.5 * skew

    for side in sides:
        for has, copy in lone_copies(side, True):
            @pl.when(has)
            def _():
                copy.wait_recv()

    def begin(q):
        for has, copy in raw_copies(q, True):
            @pl.when(has)
            def _():
                copy.wait_recv()
        for g in range(1, groups):
            prepare(0, g, q)
        for x in range(X):
            prepare(x, 0, q)
        for side in sides:
            @pl.when(has_x[side])
            def _():
                prepare_halo_x(side, q)

            @pl.when(has_y[side])
            def _():
                prepare_halo_y(side, q)

    def second(q):
        update_all(1, omega_of(STEPS - 1 - 2 % STEPS), q)
        start_sends(0, 1, q)

    begin(0)
    for q in range(chunks):
        if q + 1 < chunks:
            begin(q + 1)
        update_all(0, omega_of(STEPS - 1 - 1 % STEPS), q, 1)
        start_sends(0, 0, q)
        if q > 0:
            second(q - 1)
    second(chunks - 1)

    def round_body(number, carry):
        par = number % 2
        more = number < rounds - 1
        omega = omega_at(2 * number + 2)
        omega_even = omega_at(2 * number + 3)
        omega_odd = omega_at(2 * number + 4)

        def own(q):
            wait_arrivals(par, 0, q)
            wait_sends(1, q)
            complete_own(par, omega, q)

        def odd(q):
            @pl.when(more)
            def _():
                update_all(1, omega_odd, q)

            start_sends(1 - par, 1, q, more)

        own(0)
        for q in range(chunks):
            if q + 1 < chunks:
                own(q + 1)
            wait_arrivals(par, 1, q)
            complete_halo(par, omega, q)
            wait_sends(0, q)
            update_all(0, omega_even, q, par)
            start_sends(1 - par, 0, q, more)
            if q > 0:
                odd(q - 1)
        odd(chunks - 1)
        return carry

    lax.fori_loop(0, rounds, round_body, 0)
    for side in sides:
        for has, copy in lone_copies(side, False):
            @pl.when(has)
            def _():
                copy.wait_send()
    for q in range(chunks):
        for has, copy in raw_copies(q, False):
            @pl.when(has)
            def _():
                copy.wait_send()

    for x in range(X):
        for b in range(blocks):
            start = (x * blocks + b) * Y
            value = state[0, x, :, b * LANES : (b + 1) * LANES]
            flat[start : start + Y, :] = value
            out_ref[x, :, b * LANES : (b + 1) * LANES] = value

    @pl.loop(0, tiles // UNROLL)
    def _(part):
        for lane in range(UNROLL):
            t = part * UNROLL + lane
            picked[pl.ds(t, 1), :] = flat[pl.ds(spots_ref[t], 1), :]

    jumps = picked[...] * mask_ref[...].astype(jnp.float32)
    send_rows[...] = picked_sum(place[...], jumps).reshape(peers, CAP, LANES)

    @pl.loop(1, peers)
    def _(step):
        row_copy(step).start()

    recv_rows[me] = send_rows[me]

    @pl.loop(1, peers)
    def _(step):
        peer, place_of = peer_at(step)
        pltpu.make_async_remote_copy(
            send_slots.at[peer], recv_slots.at[peer], slot_send.at[peer], slot_recv.at[peer],
            device_id=place_of, device_id_type=MESH).wait()

    own = lax.broadcasted_iota(jnp.int32, (peers, CAP, LANES), 1)
    lane_ids = lax.broadcasted_iota(jnp.int32, (peers, CAP, LANES), 2)
    got = jnp.broadcast_to(recv_slots[...], (peers, CAP, LANES))
    slot_of = jnp.sum(jnp.where(own == lane_ids, got, 0.0), axis=2, keepdims=True)
    slot_of = slot_of.reshape(peers * CAP, 1)
    slot_ids = lax.broadcasted_iota(jnp.int32, (peers * CAP, slots), 1).astype(jnp.float32)
    chosen[...] = (slot_of == slot_ids).astype(jnp.float32).T.astype(jnp.bfloat16)

    @pl.loop(1, peers)
    def _(step):
        peer, place_of = peer_at(step)
        pltpu.make_async_remote_copy(
            send_rows.at[peer], recv_rows.at[peer], row_send.at[peer], row_recv.at[peer],
            device_id=place_of, device_id_type=MESH).wait()

    table = picked_sum(chosen[...], recv_rows[...].reshape(peers * CAP, LANES))
    for index in range(3):
        back_ref[index] = table * scales[index]


def hand_over(first_held, second_held, first_out, second_out, sem):
    stores = []
    for held, landing in ((first_held, first_out), (second_held, second_out)):
        for index in range(held.shape[0]):
            stores.append(pltpu.make_async_copy(held.at[index], landing.at[index], sem.at[len(stores)]))
    for store in stores:
        store.start()
    for store in stores:
        store.wait()


def shards(grad_pressure, beta, tile_rows, tile_owner, tile_slot, face_mask, heights):
    n_x, n_y = lax.axis_size("gx"), lax.axis_size("gy")
    peers = n_x * n_y
    X, Y, Z = grad_pressure.shape
    chunks = Z // WIDE
    tiles = tile_rows.shape[0]
    f32 = jnp.float32
    vmem = pl.BlockSpec(memory_space=pltpu.VMEM)
    hbm = pl.BlockSpec(memory_space=pltpu.HBM)
    dma = pltpu.SemaphoreType.DMA
    results = pl.pallas_call(
        functools.partial(kernel, n_x, n_y),
        out_shape=(pltpu.VMEM((X, Y, Z), f32), pltpu.VMEM(heights.shape, f32)),
        in_specs=[hbm] * 7,
        out_specs=(vmem, vmem),
        scratch_shapes=[
            pltpu.VMEM((X, Y, Z), f32),
            pltpu.VMEM(beta.shape, f32),
            pltpu.SMEM((tiles,), jnp.int32),
            pltpu.VMEM((1, tiles), jnp.int32),
            pltpu.VMEM((1, tiles), jnp.int32),
            pltpu.VMEM(face_mask.shape, jnp.int32),
            pltpu.VMEM(heights.shape, f32),
            dma((8,)),
            pltpu.VMEM((6, X, Y, Z), f32),
            pltpu.VMEM((X, Y, Z), f32),
            pltpu.VMEM((2, X, Y, Z), f32),
            pltpu.VMEM((2, 2, X, Z), f32),
            pltpu.VMEM((2, 2, 1, Z), f32),
            pltpu.VMEM((2, 2, 2, Y, Z), f32),
            pltpu.VMEM((2, 2, 2, X, Z), f32),
            pltpu.VMEM((2, 2, 2, 1, Z), f32),
            pltpu.VMEM((Y, Z), f32),
            pltpu.VMEM((X, Z), f32),
            pltpu.VMEM((X, Z), f32),
            pltpu.VMEM((2, X, Z), f32),
            pltpu.VMEM((2, Y, Z), f32),
            pltpu.VMEM((2, X, Z), f32),
            pltpu.VMEM((2, 2, 1, Z), f32),
            pltpu.VMEM((2, 2, 1, Z), f32),
            pltpu.VMEM((2, Y, Z), f32),
            pltpu.VMEM((2, X, Z), f32),
            pltpu.VMEM((2, X, Z), f32),
            pltpu.VMEM((2, 1, Z), f32),
            pltpu.VMEM((2, 1, Z), f32),
            pltpu.VMEM((2, 2, 2, 1, Z), f32),
            pltpu.VMEM((2, 2, Y, Z), f32),
            pltpu.VMEM((2, 2, X, Z), f32),
            pltpu.VMEM((2, 1, Z), f32),
            pltpu.VMEM((2, 1, Z), f32),
            pltpu.VMEM((2, 2, 2, 1, Z), f32),
            pltpu.VMEM((X * Y * Z // LANES, LANES), f32),
            pltpu.VMEM((tiles, LANES), f32),
            pltpu.SMEM((tiles,), jnp.int32),
            pltpu.VMEM((heights.shape[1], peers * CAP), jnp.bfloat16),
            pltpu.VMEM(heights.shape, f32),
            pltpu.VMEM((peers * CAP, tiles), jnp.bfloat16),
            pltpu.VMEM((peers, CAP, LANES), f32),
            pltpu.VMEM((peers, CAP, LANES), f32),
            pltpu.VMEM((peers, 1, LANES), f32),
            pltpu.VMEM((peers, 1, LANES), f32),
            dma((2, 2, chunks)),
            dma((2, 2, 2, chunks)),
            dma((2, 2, chunks)),
            dma((2, 2, 2, chunks)),
            dma((2, 2, chunks)),
            dma((2, 2, 2, chunks)),
            dma((6, 2, chunks)),
            dma((6, 2, chunks)),
            dma((4, 2)),
            dma((4, 2)),
            dma((peers,)),
            dma((peers,)),
            dma((peers,)),
            dma((peers,)),
        ],
        compiler_params=pltpu.CompilerParams(
            collective_id=0, has_side_effects=True, vmem_limit_bytes=60 * 1024 * 1024
        ),
    )(grad_pressure, beta, tile_rows, tile_owner.reshape(1, -1), tile_slot.reshape(1, -1), face_mask, heights)
    parts = sum(result.shape[0] for result in results)
    return pl.pallas_call(
        hand_over,
        out_shape=tuple(jax.ShapeDtypeStruct(result.shape, f32) for result in results),
        in_specs=[vmem] * 2,
        out_specs=(hbm, hbm),
        scratch_shapes=[dma((parts,))],
    )(*[pltpu.with_memory_space_constraint(result, pltpu.VMEM) for result in results])


def solution(mesh):
    in_specs = (
        P("gx", "gy", None),
        P(None, "gx", "gy", None),
        P(("gx", "gy")),
        P(("gx", "gy"), None),
        P(("gx", "gy")),
        P(("gx", "gy"), None),
        P(None, ("gx", "gy"), None),
    )
    out_specs = (P("gx", "gy", None), P(None, ("gx", "gy"), None))
    return jax.shard_map(shards, mesh=mesh, in_specs=in_specs, out_specs=out_specs, check_vma=False)
```

```python
import functools
import math

import jax
import jax.numpy as jnp
from jax import lax
from jax.experimental import pallas as pl
from jax.experimental.pallas import tpu as pltpu
from jax.sharding import PartitionSpec as P

ITERS = 3
STEPS = 4
CAP = 8
LANES = 128
ROWS = 8
UNROLL = 16
WIDE = 256

LOW_BOUND = 0.1
HIGH_BOUND = 1.9

MESH = pl.DeviceIdType.MESH
EXACT = lax.Precision.HIGHEST


def omega_of(step_index):
    theta = 0.5 * (HIGH_BOUND + LOW_BOUND) + 0.5 * (HIGH_BOUND - LOW_BOUND) * math.cos(
        math.pi * (2 * step_index + 1) / (2 * STEPS)
    )
    return 1.0 / theta


def omega_at(step):
    j = STEPS - 1 - step % STEPS
    value = jnp.float32(omega_of(0))
    for index in range(1, STEPS):
        value = jnp.where(j == index, jnp.float32(omega_of(index)), value)
    return value


def picked_sum(selector, rows):
    high = rows.astype(jnp.bfloat16)
    rest = rows - high.astype(jnp.float32)
    middle = rest.astype(jnp.bfloat16)
    low = (rest - middle.astype(jnp.float32)).astype(jnp.bfloat16)
    parts = [jnp.dot(selector, part, preferred_element_type=jnp.float32) for part in (high, middle, low)]
    return parts[0] + (parts[1] + parts[2])


def kernel(
    n_x, n_y,
    grad_in, beta_in, rows_in, owner_in, slot_in, mask_in, heights_in,
    out_ref, back_ref,
    grad_ref, beta_ref, rows_ref, owner_ref, slot_ref, mask_ref, heights_ref, load_sem,
    coeff, target, state, face_y, corner, halo_x, halo_y, halo_d,
    rim_x, rim_y, rim_face, face_coeff, edge_x, edge_y, line_x, line_y,
    part_x, part_y, grad_y, near_x, near_y, near_d, raw_x, raw_y, raw_by, raw_bx, raw_d,
    flat, picked, spots_ref, chosen, scales, place, send_rows, recv_rows, send_slots, recv_slots,
    x_send, x_recv, y_send, y_recv, d_send, d_recv,
    raw_send, raw_recv, lone_send, lone_recv, row_send, row_recv, slot_send, slot_recv,
):
    X, Y, Z = grad_ref.shape
    groups = Y // ROWS
    blocks = Z // LANES
    chunks = Z // WIDE
    tiles = rows_ref.shape[0]
    peers = n_x * n_y
    slots = heights_ref.shape[1]
    ix = lax.axis_index("gx")
    iy = lax.axis_index("gy")
    me = ix * n_y + iy
    has_x = (ix > 0, ix < n_x - 1)
    has_y = (iy > 0, iy < n_y - 1)
    at_x = ((ix - 1, iy), (ix + 1, iy))
    at_y = ((ix, iy - 1), (ix, iy + 1))
    sides = (0, 1)
    total = ITERS * STEPS
    rounds = (total - 2) // 2

    names = ("beta", "grad", "owner", "slot", "rows", "mask", "heights")
    pairs = (
        (beta_in, beta_ref), (grad_in, grad_ref), (owner_in, owner_ref), (slot_in, slot_ref),
        (rows_in, rows_ref), (mask_in, mask_ref), (heights_in, heights_ref),
    )
    loads = {
        name: pltpu.make_async_copy(source, held, load_sem.at[index])
        for index, (name, (source, held)) in enumerate(zip(names, pairs))
    }
    for name in names:
        loads[name].start()
    for ref in (rim_x, rim_y, halo_x, halo_y, halo_d, edge_x, edge_y, line_x, line_y, raw_d):
        ref[...] = jnp.zeros_like(ref)

    def peer_at(step):
        peer = (me + step) % peers
        return peer, (peer // n_y, peer % n_y)

    barrier = pltpu.get_barrier_semaphore()

    @pl.loop(1, peers, unroll=True)
    def _(step):
        pl.semaphore_signal(barrier, inc=1, device_id=peer_at(step)[1], device_id_type=MESH)

    z_ids = lax.broadcasted_iota(jnp.int32, (ROWS, Z), 1)

    def row_index(width):
        return lax.broadcasted_iota(jnp.int32, (ROWS, width), 0)

    def from_below(tile, row):
        return jnp.where(row_index(tile.shape[1]) == 0, row, pltpu.roll(tile, 1, 0))

    def from_above(tile, row):
        return jnp.where(row_index(tile.shape[1]) == ROWS - 1, row, pltpu.roll(tile, ROWS - 1, 0))

    def part_of_diagonal(x, g):
        r = slice(g * ROWS, (g + 1) * ROWS)
        up_y, up_z = beta_ref[1, x, r, :], beta_ref[2, x, r, :]
        low_y = from_below(up_y, 0.0 if g == 0 else beta_ref[1, x, g * ROWS - 1 : g * ROWS, :])
        value = beta_ref[0, x, r, :] + up_y + low_y + up_z + jnp.where(z_ids == 0, 0.0, pltpu.roll(up_z, 1, 1))
        return value if x == 0 else value + beta_ref[0, x - 1, r, :]

    loads["beta"].wait()
    for x in range(X):
        rim_face[x : x + 1, :] = beta_ref[1, x, Y - 1 : Y, :]
        for g in range(groups):
            if x in (0, X - 1) or g in (0, groups - 1):
                value = part_of_diagonal(x, g)
                if x in (0, X - 1):
                    part_x[0 if x == 0 else 1, g * ROWS : (g + 1) * ROWS, :] = value
                if g == 0:
                    part_y[0, x : x + 1, :] = value[:1, :]
                if g == groups - 1:
                    part_y[1, x : x + 1, :] = value[ROWS - 1 :, :]
    for side in sides:
        near_x[side] = beta_ref[1, (X - 1) * side, Y - 1 : Y, :]
        near_y[side] = beta_ref[0, X - 1, (Y - 1) * side : (Y - 1) * side + 1, :]
        for dy in sides:
            near_d[side, dy, 0] = beta_ref[0, X - 1, (Y - 1) * dy : (Y - 1) * dy + 1, :]
            near_d[side, dy, 1] = beta_ref[1, (X - 1) * side, Y - 1 : Y, :]
    loads["grad"].wait()
    for x in range(X):
        for side in sides:
            grad_y[side, x : x + 1, :] = grad_ref[x, (Y - 1) * side : (Y - 1) * side + 1, :]

    pl.semaphore_wait(barrier, peers - 1)

    def remote(source, landing, send, recv, place_of):
        return pltpu.make_async_remote_copy(source, landing, send, recv, device_id=place_of, device_id_type=MESH)

    def slot_copy(step):
        peer, place_of = peer_at(step)
        return pltpu.make_async_remote_copy(
            send_slots.at[peer], recv_slots.at[me], slot_send.at[peer], slot_recv.at[me],
            device_id=place_of, device_id_type=MESH)

    def row_copy(step):
        peer, place_of = peer_at(step)
        return pltpu.make_async_remote_copy(
            send_rows.at[peer], recv_rows.at[me], row_send.at[peer], row_recv.at[me],
            device_id=place_of, device_id_type=MESH)

    def reach(kind, q):
        if kind == 0:
            return q * WIDE, (q + 1) * WIDE
        return max(q * WIDE - LANES, 0), ((q + 1) * WIDE - LANES if q < chunks - 1 else Z)

    def lanes(q, kind=0):
        start, stop = reach(kind, q)
        return pl.ds(start, stop - start)

    def x_copy(par, kind, side, q, land):
        return remote(
            state.at[kind, (X - 1) * side, :, lanes(q, kind)], halo_x.at[par, kind, land, :, lanes(q, kind)],
            x_send.at[kind, side, q], x_recv.at[par, kind, land, q], at_x[side])

    def y_copy(par, kind, side, q, land):
        return remote(
            face_y.at[kind, side, :, lanes(q, kind)], halo_y.at[par, kind, land, :, lanes(q, kind)],
            y_send.at[kind, side, q], y_recv.at[par, kind, land, q], (ix, iy + 2 * side - 1))

    def d_copy(par, dx, dy, q, land):
        return remote(
            corner.at[dx, dy, :, lanes(q)], halo_d.at[par, land[0], land[1], :, lanes(q)],
            d_send.at[dx, dy, q], d_recv.at[par, land[0], land[1], q], (at_x[dx][0], at_y[dy][1]))

    def each_side(act_x, act_y):
        for side in sides:
            @pl.when(has_x[side])
            def _():
                act_x(side)

            @pl.when(has_y[side])
            def _():
                act_y(side)

    def each_corner(act):
        for dx in sides:
            for dy in sides:
                @pl.when(jnp.logical_and(has_x[dx], has_y[dy]))
                def _():
                    act(dx, dy)

    def start_sends(par, kind, q):
        for turn in sides:
            side = (iy + turn) % 2

            @pl.when(jnp.logical_and(iy + 2 * side - 1 >= 0, iy + 2 * side - 1 < n_y))
            def _():
                y_copy(par, kind, side, q, 1 - side).start()

        if kind == 0:
            each_corner(lambda dx, dy: d_copy(par, dx, dy, q, (1 - dx, 1 - dy)).start())
        for side in sides:
            @pl.when(has_x[side])
            def _():
                x_copy(par, kind, side, q, 1 - side).start()

    def coming(q):
        return [at for at in ((0, 1) if q == 0 else (q + 1,)) if at < chunks]

    def wait_own(par, q):
        def x_side(side):
            x_copy(par, 0, side, q, side).wait_recv()
            for at in coming(q):
                x_copy(par, 1, side, at, 1 - side).wait_send()

        def y_side(side):
            y_copy(par, 0, side, q, side).wait_recv()
            for at in coming(q):
                y_copy(par, 1, side, at, 1 - side).wait_send()

        def at_corner(dx, dy):
            d_copy(par, dx, dy, q, (dx, dy)).wait_recv()
            d_copy(par, dx, dy, q, (1 - dx, 1 - dy)).wait_send()

        each_side(x_side, y_side)
        each_corner(at_corner)

    def wait_halo(par, q):
        def x_side(side):
            for at in coming(q):
                x_copy(par, 1, side, at, side).wait_recv()
            x_copy(par, 0, side, q, 1 - side).wait_send()

        def y_side(side):
            for at in coming(q):
                y_copy(par, 1, side, at, side).wait_recv()
            y_copy(par, 0, side, q, 1 - side).wait_send()

        each_side(x_side, y_side)

    def lone_copies(side, arriving):
        land = side if arriving else 1 - side
        found = [
            (has_x[side], remote(near_x.at[side], raw_by.at[land], lone_send.at[0, side], lone_recv.at[0, land], at_x[side])),
            (has_y[side], remote(near_y.at[side], raw_bx.at[land], lone_send.at[1, side], lone_recv.at[1, land], at_y[side])),
        ]
        for dy in sides:
            other = dy if arriving else 1 - dy
            found.append((jnp.logical_and(has_x[side], has_y[dy]), remote(
                near_d.at[side, dy], raw_d.at[land, other], lone_send.at[2 + dy, side], lone_recv.at[2 + other, land],
                (at_x[side][0], at_y[dy][1]))))
        return found

    def raw_copies(q, arriving):
        cut = lanes(q)
        found = []
        for side in sides:
            land = side if arriving else 1 - side
            sources = (
                (has_x, at_x, 0, beta_ref.at[0, X - 1, :, cut], rim_x.at[:, cut]),
                (has_y, at_y, 1, rim_face.at[:, cut], rim_y.at[:, cut]),
                (has_x, at_x, 2, grad_ref.at[(X - 1) * side, :, cut], raw_x.at[0, land, :, cut]),
                (has_y, at_y, 3, grad_y.at[side, :, cut], raw_y.at[0, land, :, cut]),
                (has_x, at_x, 4, part_x.at[side, :, cut], raw_x.at[1, land, :, cut]),
                (has_y, at_y, 5, part_y.at[side, :, cut], raw_y.at[1, land, :, cut]),
            )
            for has, at, kind, source, landing in sources:
                if kind > 1 or side == (0 if arriving else 1):
                    found.append((has[side], remote(
                        source, landing, raw_send.at[kind, side, q], raw_recv.at[kind, land, q], at[side])))
        return found

    first = omega_of(STEPS - 1)

    def keep_faces(kind, value, x, g, cut):
        if g == 0:
            face_y[kind, 0, x : x + 1, cut] = value[:1, :]
        if g == groups - 1:
            face_y[kind, 1, x : x + 1, cut] = value[ROWS - 1 :, :]
        if kind == 0 and x in (0, X - 1):
            if g == 0:
                corner[0 if x == 0 else 1, 0, :, cut] = value[:1, :]
            if g == groups - 1:
                corner[0 if x == 0 else 1, 1, :, cut] = value[ROWS - 1 :, :]

    def prepare(x, g, q=None):
        r = slice(g * ROWS, (g + 1) * ROWS)
        start, stop = (0, Z) if q is None else (q * WIDE, (q + 1) * WIDE)
        cut = slice(start, stop)
        wide = slice(max(start - LANES, 0), stop)
        inner = slice(start - wide.start, stop - wide.start)
        z_at = z_ids[:, cut]
        up_x, up_y, up_z = beta_ref[0, x, r, cut], beta_ref[1, x, r, cut], beta_ref[2, x, r, wide]
        low_x = rim_x[r, cut] if x == 0 else beta_ref[0, x - 1, r, cut]
        row = rim_y[x : x + 1, cut] if g == 0 else beta_ref[1, x, g * ROWS - 1 : g * ROWS, cut]
        low_y = from_below(up_y, row)
        low_z = jnp.where(z_at == 0, 0.0, pltpu.roll(up_z, 1, 1)[:, inner])
        up_z = up_z[:, inner]
        inv = 1.0 / (up_x + low_x + up_y + low_y + up_z + low_z)
        up_z = jnp.where(z_at == Z - 1, 0.0, up_z)
        for index, value in enumerate((up_x, low_x, up_y, low_y, up_z, low_z)):
            value = value * inv
            coeff[index, x, r, cut] = value
            if index == 3 and g == 0:
                face_coeff[0, x : x + 1, cut] = value[:1, :]
            if index == 2 and g == groups - 1:
                face_coeff[1, x : x + 1, cut] = value[ROWS - 1 :, :]
        value = inv * grad_ref[x, r, cut]
        target[x, r, cut] = value
        state[1, x, r, cut] = first * value

    def prepare_halo_x(side, q):
        cut = slice(q * WIDE, (q + 1) * WIDE)
        for g in range(groups):
            r = slice(g * ROWS, (g + 1) * ROWS)
            shared = beta_ref[0, X - 1, r, cut] if side else rim_x[r, cut]
            total_of = raw_x[1, side, r, cut]
            if side:
                total_of += shared
            if g == 0:
                total_of += jnp.where(row_index(WIDE) == 0, raw_d[side, 0, 1, :, cut], 0.0)
            inv = 1.0 / total_of
            halo_x[1, 1, side, r, cut] = first * (inv * raw_x[0, side, r, cut])
            edge_x[side, r, cut] = shared * inv
            if g == 0:
                line_x[side, 0, :, cut] = raw_d[side, 0, 1, :, cut] * inv[:1, :]
            if g == groups - 1:
                line_x[side, 1, :, cut] = raw_by[side, :, cut] * inv[ROWS - 1 :, :]

    def prepare_halo_y(side, q):
        cut = slice(q * WIDE, (q + 1) * WIDE)
        shared = rim_face[:, cut] if side else rim_y[:, cut]
        total_of = raw_y[1, side, :, cut]
        if side:
            total_of += shared
        planes = lax.broadcasted_iota(jnp.int32, (X, WIDE), 0)
        total_of += jnp.where(planes == 0, raw_d[0, side, 0, :, cut], 0.0)
        inv = 1.0 / total_of
        halo_y[1, 1, side, :, cut] = first * (inv * raw_y[0, side, :, cut])
        edge_y[side, :, cut] = shared * inv
        line_y[side, 0, :, cut] = raw_d[0, side, 0, :, cut] * inv[:1, :]
        line_y[side, 1, :, cut] = raw_bx[side, :, cut] * inv[X - 1 :, :]

    def update_all(kind, omega, q, par=None):
        source = 1 - kind
        low, high = reach(kind, q)
        cut = slice(low, high)
        start, stop = max(low - LANES, 0), min(high + LANES, Z)
        inner = slice(low - start, high - start)
        rows = [slice(g * ROWS, (g + 1) * ROWS) for g in range(groups)]
        at_top, at_bottom = row_index(high - low) == ROWS - 1, row_index(high - low) == 0

        def plane(x):
            return [state[source, x, r, start:stop] for r in rows]

        before, here, after = None, plane(0), None
        for x in range(X):
            after = plane(x + 1) if x < X - 1 else None
            middle = [tile[:, inner] for tile in here]
            ups = [pltpu.roll(tile, ROWS - 1, 0) for tile in middle]
            downs = [pltpu.roll(tile, 1, 0) for tile in middle]
            edges = [0.0, 0.0] if par is None else [halo_y[par, 1, side, x : x + 1, cut] for side in sides]
            for g, r in enumerate(rows):
                s = middle[g]
                beside = target[x, r, cut] - s
                beside += coeff[2, x, r, cut] * jnp.where(at_top, ups[g + 1] if g < groups - 1 else edges[1], ups[g])
                beside += coeff[3, x, r, cut] * jnp.where(at_bottom, downs[g - 1] if g > 0 else edges[0], downs[g])
                beside += coeff[4, x, r, cut] * pltpu.roll(here[g], stop - start - 1, 1)[:, inner]
                beside += coeff[5, x, r, cut] * pltpu.roll(here[g], 1, 1)[:, inner]
                if x < X - 1:
                    beside += coeff[0, x, r, cut] * after[g][:, inner]
                elif par is not None:
                    beside += coeff[0, x, r, cut] * halo_x[par, 1, 1, r, cut]
                if x > 0:
                    beside += coeff[1, x, r, cut] * before[g]
                elif par is not None:
                    beside += coeff[1, x, r, cut] * halo_x[par, 1, 0, r, cut]
                value = s + omega * beside
                state[kind, x, r, cut] = value
                keep_faces(kind, value, x, g, cut)
            before, here = middle, after

    def complete_own(par, omega, q):
        cut = slice(q * WIDE, (q + 1) * WIDE)
        for side in sides:
            x = (X - 1) * side
            for g in range(groups):
                r = slice(g * ROWS, (g + 1) * ROWS)
                state[1, x, r, cut] += omega * (coeff[1 - side, x, r, cut] * halo_x[par, 0, side, r, cut])
        for side in sides:
            more = omega * (face_coeff[side, :, cut] * halo_y[par, 0, side, :, cut])
            row = (Y - 1) * side
            for x in range(X):
                state[1, x, row : row + 1, cut] += more[x : x + 1, :]

    def complete_halo(par, omega, q):
        cut = slice(*reach(1, q))
        for side in sides:
            x = (X - 1) * side
            for g in range(groups):
                r = slice(g * ROWS, (g + 1) * ROWS)
                halo_x[par, 1, side, r, cut] += omega * (edge_x[side, r, cut] * state[0, x, r, cut])
            for dy in sides:
                row = (Y - 1) * dy
                halo_x[par, 1, side, row : row + 1, cut] += omega * (
                    line_x[side, dy, :, cut] * halo_d[par, side, dy, :, cut])
        for side in sides:
            halo_y[par, 1, side, :, cut] += omega * (edge_y[side, :, cut] * face_y[0, side, :, cut])
            for dx in sides:
                x = (X - 1) * dx
                halo_y[par, 1, side, x : x + 1, cut] += omega * (
                    line_y[side, dx, :, cut] * halo_d[par, dx, side, :, cut])

    for side in sides:
        for has, copy in lone_copies(side, False):
            @pl.when(has)
            def _():
                copy.start()
    for q in range(chunks):
        for has, copy in raw_copies(q, False):
            @pl.when(has)
            def _():
                copy.start()

    for name in ("owner", "slot"):
        loads[name].wait()

    owner = owner_ref[...]
    peer_ids = lax.broadcasted_iota(jnp.int32, (peers, tiles), 0)
    named = (owner == peer_ids).astype(jnp.float32)
    down = lax.broadcasted_iota(jnp.int32, (tiles, tiles), 0)
    across = lax.broadcasted_iota(jnp.int32, (tiles, tiles), 1)
    earlier = (down < across).astype(jnp.bfloat16)
    counts = jnp.dot(named.astype(jnp.bfloat16), earlier, preferred_element_type=jnp.float32)
    position = jnp.sum(counts * named, axis=0, keepdims=True)
    spot = owner.astype(jnp.float32) * CAP + position
    spots = lax.broadcasted_iota(jnp.int32, (peers * CAP, tiles), 0).astype(jnp.float32)
    place[...] = (spot == spots).astype(jnp.float32).astype(jnp.bfloat16)
    spread = lax.broadcasted_iota(jnp.int32, (LANES, tiles), 0).astype(jnp.float32)
    spread = (spread == position).astype(jnp.float32)
    slot_rows = lax.dot_general(
        named * slot_ref[...].astype(jnp.float32), spread, (((1,), (1,)), ((), ())),
        preferred_element_type=jnp.float32, precision=EXACT,
    )
    send_slots[...] = slot_rows.reshape(peers, 1, LANES)

    @pl.loop(1, peers, unroll=True)
    def _(step):
        slot_copy(step).start()

    recv_slots[me] = send_slots[me]
    for x in range(1, X):
        for g in range(1, groups):
            prepare(x, g)

    for name in ("rows", "mask", "heights"):
        loads[name].wait()

    @pl.loop(0, tiles // UNROLL)
    def _(part):
        for lane in range(UNROLL):
            t = part * UNROLL + lane
            row = rows_ref[t]
            line = lax.div(row, blocks)
            x = lax.div(line, Y)
            spots_ref[t] = (x * blocks + row - line * blocks) * Y + line - x * Y

    slope = 0.5 * (heights_ref[2] - heights_ref[0])
    bend = heights_ref[2] - 2.0 * heights_ref[1] + heights_ref[0]
    denom = 1.0 + slope * slope
    factor = 1.0 / (denom * jnp.sqrt(denom))
    skew = -3.0 * slope * bend * factor / denom
    scales[0] = factor - 0.5 * skew
    scales[1] = -2.0 * factor
    scales[2] = factor + 0.5 * skew

    for side in sides:
        for has, copy in lone_copies(side, True):
            @pl.when(has)
            def _():
                copy.wait_recv()

    def begin(q):
        for has, copy in raw_copies(q, True):
            @pl.when(has)
            def _():
                copy.wait_recv()
        for g in range(1, groups):
            prepare(0, g, q)
        for x in range(X):
            prepare(x, 0, q)
        for side in sides:
            @pl.when(has_x[side])
            def _():
                prepare_halo_x(side, q)

            @pl.when(has_y[side])
            def _():
                prepare_halo_y(side, q)

    def second(q):
        update_all(1, omega_of(STEPS - 1 - 2 % STEPS), q)
        start_sends(0, 1, q)

    begin(0)
    for q in range(chunks):
        if q + 1 < chunks:
            begin(q + 1)
        update_all(0, omega_of(STEPS - 1 - 1 % STEPS), q, 1)
        start_sends(0, 0, q)
        second(q)

    def round_body(number, carry):
        par = number % 2
        more = number < rounds - 1
        omega = omega_at(2 * number + 2)
        omega_even = omega_at(2 * number + 3)
        omega_odd = omega_at(2 * number + 4)

        def own(q):
            wait_own(par, q)
            complete_own(par, omega, q)

        def odd(q):
            @pl.when(more)
            def _():
                update_all(1, omega_odd, q)
                start_sends(1 - par, 1, q)

        own(0)
        for q in range(chunks):
            if q + 1 < chunks:
                own(q + 1)
            wait_halo(par, q)
            for at in coming(q):
                complete_halo(par, omega, at)
            update_all(0, omega_even, q, par)

            @pl.when(more)
            def _():
                start_sends(1 - par, 0, q)

            odd(q)
        return carry

    lax.fori_loop(0, rounds, round_body, 0)
    for side in sides:
        for has, copy in lone_copies(side, False):
            @pl.when(has)
            def _():
                copy.wait_send()
    for q in range(chunks):
        for has, copy in raw_copies(q, False):
            @pl.when(has)
            def _():
                copy.wait_send()

    for x in range(X):
        for b in range(blocks):
            start = (x * blocks + b) * Y
            value = state[0, x, :, b * LANES : (b + 1) * LANES]
            flat[start : start + Y, :] = value
            out_ref[x, :, b * LANES : (b + 1) * LANES] = value

    @pl.loop(0, tiles // UNROLL)
    def _(part):
        for lane in range(UNROLL):
            t = part * UNROLL + lane
            picked[pl.ds(t, 1), :] = flat[pl.ds(spots_ref[t], 1), :]

    jumps = picked[...] * mask_ref[...].astype(jnp.float32)
    send_rows[...] = picked_sum(place[...], jumps).reshape(peers, CAP, LANES)

    @pl.loop(1, peers, unroll=True)
    def _(step):
        row_copy(step).start()

    recv_rows[me] = send_rows[me]

    @pl.loop(1, peers, unroll=True)
    def _(step):
        peer, place_of = peer_at(step)
        pltpu.make_async_remote_copy(
            send_slots.at[peer], recv_slots.at[peer], slot_send.at[peer], slot_recv.at[peer],
            device_id=place_of, device_id_type=MESH).wait()

    own = lax.broadcasted_iota(jnp.int32, (peers, CAP, LANES), 1)
    lane_ids = lax.broadcasted_iota(jnp.int32, (peers, CAP, LANES), 2)
    got = jnp.broadcast_to(recv_slots[...], (peers, CAP, LANES))
    slot_of = jnp.sum(jnp.where(own == lane_ids, got, 0.0), axis=2, keepdims=True)
    slot_of = slot_of.reshape(peers * CAP, 1)
    slot_ids = lax.broadcasted_iota(jnp.int32, (peers * CAP, slots), 1).astype(jnp.float32)
    chosen[...] = (slot_of == slot_ids).astype(jnp.float32).T.astype(jnp.bfloat16)

    @pl.loop(1, peers, unroll=True)
    def _(step):
        peer, place_of = peer_at(step)
        pltpu.make_async_remote_copy(
            send_rows.at[peer], recv_rows.at[peer], row_send.at[peer], row_recv.at[peer],
            device_id=place_of, device_id_type=MESH).wait()

    table = picked_sum(chosen[...], recv_rows[...].reshape(peers * CAP, LANES))
    for index in range(3):
        back_ref[index] = table * scales[index]


def hand_over(first_held, second_held, first_out, second_out, sem):
    stores = []
    for held, landing in ((first_held, first_out), (second_held, second_out)):
        for index in range(held.shape[0]):
            stores.append(pltpu.make_async_copy(held.at[index], landing.at[index], sem.at[len(stores)]))
    for store in stores:
        store.start()
    for store in stores:
        store.wait()


def shards(grad_pressure, beta, tile_rows, tile_owner, tile_slot, face_mask, heights):
    n_x, n_y = lax.axis_size("gx"), lax.axis_size("gy")
    peers = n_x * n_y
    X, Y, Z = grad_pressure.shape
    chunks = Z // WIDE
    tiles = tile_rows.shape[0]
    f32 = jnp.float32
    vmem = pl.BlockSpec(memory_space=pltpu.VMEM)
    hbm = pl.BlockSpec(memory_space=pltpu.HBM)
    dma = pltpu.SemaphoreType.DMA
    results = pl.pallas_call(
        functools.partial(kernel, n_x, n_y),
        out_shape=(pltpu.VMEM((X, Y, Z), f32), pltpu.VMEM(heights.shape, f32)),
        in_specs=[hbm] * 7,
        out_specs=(vmem, vmem),
        scratch_shapes=[
            pltpu.VMEM((X, Y, Z), f32),
            pltpu.VMEM(beta.shape, f32),
            pltpu.SMEM((tiles,), jnp.int32),
            pltpu.VMEM((1, tiles), jnp.int32),
            pltpu.VMEM((1, tiles), jnp.int32),
            pltpu.VMEM(face_mask.shape, jnp.int32),
            pltpu.VMEM(heights.shape, f32),
            dma((8,)),
            pltpu.VMEM((6, X, Y, Z), f32),
            pltpu.VMEM((X, Y, Z), f32),
            pltpu.VMEM((2, X, Y, Z), f32),
            pltpu.VMEM((2, 2, X, Z), f32),
            pltpu.VMEM((2, 2, 1, Z), f32),
            pltpu.VMEM((2, 2, 2, Y, Z), f32),
            pltpu.VMEM((2, 2, 2, X, Z), f32),
            pltpu.VMEM((2, 2, 2, 1, Z), f32),
            pltpu.VMEM((Y, Z), f32),
            pltpu.VMEM((X, Z), f32),
            pltpu.VMEM((X, Z), f32),
            pltpu.VMEM((2, X, Z), f32),
            pltpu.VMEM((2, Y, Z), f32),
            pltpu.VMEM((2, X, Z), f32),
            pltpu.VMEM((2, 2, 1, Z), f32),
            pltpu.VMEM((2, 2, 1, Z), f32),
            pltpu.VMEM((2, Y, Z), f32),
            pltpu.VMEM((2, X, Z), f32),
            pltpu.VMEM((2, X, Z), f32),
            pltpu.VMEM((2, 1, Z), f32),
            pltpu.VMEM((2, 1, Z), f32),
            pltpu.VMEM((2, 2, 2, 1, Z), f32),
            pltpu.VMEM((2, 2, Y, Z), f32),
            pltpu.VMEM((2, 2, X, Z), f32),
            pltpu.VMEM((2, 1, Z), f32),
            pltpu.VMEM((2, 1, Z), f32),
            pltpu.VMEM((2, 2, 2, 1, Z), f32),
            pltpu.VMEM((X * Y * Z // LANES, LANES), f32),
            pltpu.VMEM((tiles, LANES), f32),
            pltpu.SMEM((tiles,), jnp.int32),
            pltpu.VMEM((heights.shape[1], peers * CAP), jnp.bfloat16),
            pltpu.VMEM(heights.shape, f32),
            pltpu.VMEM((peers * CAP, tiles), jnp.bfloat16),
            pltpu.VMEM((peers, CAP, LANES), f32),
            pltpu.VMEM((peers, CAP, LANES), f32),
            pltpu.VMEM((peers, 1, LANES), f32),
            pltpu.VMEM((peers, 1, LANES), f32),
            dma((2, 2, chunks)),
            dma((2, 2, 2, chunks)),
            dma((2, 2, chunks)),
            dma((2, 2, 2, chunks)),
            dma((2, 2, chunks)),
            dma((2, 2, 2, chunks)),
            dma((6, 2, chunks)),
            dma((6, 2, chunks)),
            dma((4, 2)),
            dma((4, 2)),
            dma((peers,)),
            dma((peers,)),
            dma((peers,)),
            dma((peers,)),
        ],
        compiler_params=pltpu.CompilerParams(
            collective_id=0, has_side_effects=True, vmem_limit_bytes=60 * 1024 * 1024
        ),
    )(grad_pressure, beta, tile_rows, tile_owner.reshape(1, -1), tile_slot.reshape(1, -1), face_mask, heights)
    parts = sum(result.shape[0] for result in results)
    return pl.pallas_call(
        hand_over,
        out_shape=tuple(jax.ShapeDtypeStruct(result.shape, f32) for result in results),
        in_specs=[vmem] * 2,
        out_specs=(hbm, hbm),
        scratch_shapes=[dma((parts,))],
    )(*[pltpu.with_memory_space_constraint(result, pltpu.VMEM) for result in results])


def solution(mesh):
    in_specs = (
        P("gx", "gy", None),
        P(None, "gx", "gy", None),
        P(("gx", "gy")),
        P(("gx", "gy"), None),
        P(("gx", "gy")),
        P(("gx", "gy"), None),
        P(None, ("gx", "gy"), None),
    )
    out_specs = (P("gx", "gy", None), P(None, ("gx", "gy"), None))
    return jax.shard_map(shards, mesh=mesh, in_specs=in_specs, out_specs=out_specs, check_vma=False)
```

```python
import functools
import math

import jax
import jax.numpy as jnp
from jax import lax
from jax.experimental import pallas as pl
from jax.experimental.pallas import tpu as pltpu
from jax.sharding import PartitionSpec as P

ITERS = 3
STEPS = 4
CAP = 8
LANES = 128
ROWS = 8
UNROLL = 16
WIDE = 256

LOW_BOUND = 0.1
HIGH_BOUND = 1.9

MESH = pl.DeviceIdType.MESH
EXACT = lax.Precision.HIGHEST


def omega_of(step_index):
    theta = 0.5 * (HIGH_BOUND + LOW_BOUND) + 0.5 * (HIGH_BOUND - LOW_BOUND) * math.cos(
        math.pi * (2 * step_index + 1) / (2 * STEPS)
    )
    return 1.0 / theta


def omega_at(step):
    j = STEPS - 1 - step % STEPS
    value = jnp.float32(omega_of(0))
    for index in range(1, STEPS):
        value = jnp.where(j == index, jnp.float32(omega_of(index)), value)
    return value


def picked_sum(selector, rows):
    high = rows.astype(jnp.bfloat16)
    rest = rows - high.astype(jnp.float32)
    middle = rest.astype(jnp.bfloat16)
    low = (rest - middle.astype(jnp.float32)).astype(jnp.bfloat16)
    parts = [jnp.dot(selector, part, preferred_element_type=jnp.float32) for part in (high, middle, low)]
    return parts[0] + (parts[1] + parts[2])


def kernel(
    n_x, n_y,
    grad_in, beta_in, rows_in, owner_in, slot_in, mask_in, heights_in,
    out_ref, back_ref,
    grad_ref, beta_ref, rows_ref, owner_ref, slot_ref, mask_ref, heights_ref, load_sem,
    coeff, target, state, face_y, corner, halo_x, halo_y, halo_d,
    rim_x, rim_y, rim_face, face_coeff, edge_x, edge_y, line_x, line_y,
    part_x, part_y, grad_y, near_x, near_y, near_d, raw_x, raw_y, raw_by, raw_bx, raw_d,
    flat, picked, spots_ref, chosen, scales, place, send_rows, recv_rows, send_slots, recv_slots,
    x_send, x_recv, y_send, y_recv, d_send, d_recv,
    raw_send, raw_recv, lone_send, lone_recv, row_send, row_recv, slot_send, slot_recv,
):
    X, Y, Z = grad_ref.shape
    groups = Y // ROWS
    blocks = Z // LANES
    chunks = Z // WIDE
    tiles = rows_ref.shape[0]
    peers = n_x * n_y
    slots = heights_ref.shape[1]
    ix = lax.axis_index("gx")
    iy = lax.axis_index("gy")
    me = ix * n_y + iy
    has_x = (ix > 0, ix < n_x - 1)
    has_y = (iy > 0, iy < n_y - 1)
    at_x = ((ix - 1, iy), (ix + 1, iy))
    at_y = ((ix, iy - 1), (ix, iy + 1))
    sides = (0, 1)
    total = ITERS * STEPS
    rounds = (total - 2) // 2

    names = ("beta", "grad", "owner", "slot", "rows", "mask", "heights")
    pairs = (
        (beta_in, beta_ref), (grad_in, grad_ref), (owner_in, owner_ref), (slot_in, slot_ref),
        (rows_in, rows_ref), (mask_in, mask_ref), (heights_in, heights_ref),
    )
    loads = {
        name: pltpu.make_async_copy(source, held, load_sem.at[index])
        for index, (name, (source, held)) in enumerate(zip(names, pairs))
    }
    for name in names:
        loads[name].start()
    for ref in (rim_x, rim_y, halo_x, halo_y, halo_d, edge_x, edge_y, line_x, line_y, raw_d):
        ref[...] = jnp.zeros_like(ref)

    def peer_at(step):
        peer = (me + step) % peers
        return peer, (peer // n_y, peer % n_y)

    barrier = pltpu.get_barrier_semaphore()

    @pl.loop(1, peers, unroll=True)
    def _(step):
        pl.semaphore_signal(barrier, inc=1, device_id=peer_at(step)[1], device_id_type=MESH)

    z_ids = lax.broadcasted_iota(jnp.int32, (ROWS, Z), 1)

    def row_index(width):
        return lax.broadcasted_iota(jnp.int32, (ROWS, width), 0)

    def from_below(tile, row):
        return jnp.where(row_index(tile.shape[1]) == 0, row, pltpu.roll(tile, 1, 0))

    def from_above(tile, row):
        return jnp.where(row_index(tile.shape[1]) == ROWS - 1, row, pltpu.roll(tile, ROWS - 1, 0))

    def part_of_diagonal(x, g):
        r = slice(g * ROWS, (g + 1) * ROWS)
        up_y, up_z = beta_ref[1, x, r, :], beta_ref[2, x, r, :]
        low_y = from_below(up_y, 0.0 if g == 0 else beta_ref[1, x, g * ROWS - 1 : g * ROWS, :])
        value = beta_ref[0, x, r, :] + up_y + low_y + up_z + jnp.where(z_ids == 0, 0.0, pltpu.roll(up_z, 1, 1))
        return value if x == 0 else value + beta_ref[0, x - 1, r, :]

    loads["beta"].wait()
    for x in range(X):
        rim_face[x : x + 1, :] = beta_ref[1, x, Y - 1 : Y, :]
        for g in range(groups):
            if x in (0, X - 1) or g in (0, groups - 1):
                value = part_of_diagonal(x, g)
                if x in (0, X - 1):
                    part_x[0 if x == 0 else 1, g * ROWS : (g + 1) * ROWS, :] = value
                if g == 0:
                    part_y[0, x : x + 1, :] = value[:1, :]
                if g == groups - 1:
                    part_y[1, x : x + 1, :] = value[ROWS - 1 :, :]
    for side in sides:
        near_x[side] = beta_ref[1, (X - 1) * side, Y - 1 : Y, :]
        near_y[side] = beta_ref[0, X - 1, (Y - 1) * side : (Y - 1) * side + 1, :]
        for dy in sides:
            near_d[side, dy, 0] = beta_ref[0, X - 1, (Y - 1) * dy : (Y - 1) * dy + 1, :]
            near_d[side, dy, 1] = beta_ref[1, (X - 1) * side, Y - 1 : Y, :]
    loads["grad"].wait()
    for x in range(X):
        for side in sides:
            grad_y[side, x : x + 1, :] = grad_ref[x, (Y - 1) * side : (Y - 1) * side + 1, :]

    pl.semaphore_wait(barrier, peers - 1)

    def remote(source, landing, send, recv, place_of):
        return pltpu.make_async_remote_copy(source, landing, send, recv, device_id=place_of, device_id_type=MESH)

    def slot_copy(step):
        peer, place_of = peer_at(step)
        return pltpu.make_async_remote_copy(
            send_slots.at[peer], recv_slots.at[me], slot_send.at[peer], slot_recv.at[me],
            device_id=place_of, device_id_type=MESH)

    def row_copy(step):
        peer, place_of = peer_at(step)
        return pltpu.make_async_remote_copy(
            send_rows.at[peer], recv_rows.at[me], row_send.at[peer], row_recv.at[me],
            device_id=place_of, device_id_type=MESH)

    def reach(kind, q):
        if kind == 0:
            return q * WIDE, (q + 1) * WIDE
        return max(q * WIDE - LANES, 0), ((q + 1) * WIDE - LANES if q < chunks - 1 else Z)

    def lanes(q, kind=0):
        start, stop = reach(kind, q)
        return pl.ds(start, stop - start)

    def x_copy(par, kind, side, q, land):
        return remote(
            state.at[kind, (X - 1) * side, :, lanes(q, kind)], halo_x.at[par, kind, land, :, lanes(q, kind)],
            x_send.at[kind, side, q], x_recv.at[par, kind, land, q], at_x[side])

    def y_copy(par, kind, side, q, land):
        return remote(
            face_y.at[kind, side, :, lanes(q, kind)], halo_y.at[par, kind, land, :, lanes(q, kind)],
            y_send.at[kind, side, q], y_recv.at[par, kind, land, q], (ix, iy + 2 * side - 1))

    def d_copy(par, dx, dy, q, land):
        return remote(
            corner.at[dx, dy, :, lanes(q)], halo_d.at[par, land[0], land[1], :, lanes(q)],
            d_send.at[dx, dy, q], d_recv.at[par, land[0], land[1], q], (at_x[dx][0], at_y[dy][1]))

    def each_side(act_x, act_y):
        for side in sides:
            @pl.when(has_x[side])
            def _():
                act_x(side)

            @pl.when(has_y[side])
            def _():
                act_y(side)

    def each_corner(act):
        for dx in sides:
            for dy in sides:
                @pl.when(jnp.logical_and(has_x[dx], has_y[dy]))
                def _():
                    act(dx, dy)

    def start_sends(par, kind, q):
        if kind == 0:
            each_corner(lambda dx, dy: d_copy(par, dx, dy, q, (1 - dx, 1 - dy)).start())
        for turn in sides:
            side = (iy + turn) % 2

            @pl.when(jnp.logical_and(iy + 2 * side - 1 >= 0, iy + 2 * side - 1 < n_y))
            def _():
                y_copy(par, kind, side, q, 1 - side).start()

        for side in sides:
            @pl.when(has_x[side])
            def _():
                x_copy(par, kind, side, q, 1 - side).start()

    def coming(q):
        return [at for at in ((0, 1) if q == 0 else (q + 1,)) if at < chunks]

    def wait_own(par, q):
        def x_side(side):
            x_copy(par, 0, side, q, side).wait_recv()
            for at in coming(q):
                x_copy(par, 1, side, at, 1 - side).wait_send()

        def y_side(side):
            y_copy(par, 0, side, q, side).wait_recv()
            for at in coming(q):
                y_copy(par, 1, side, at, 1 - side).wait_send()

        def at_corner(dx, dy):
            d_copy(par, dx, dy, q, (dx, dy)).wait_recv()
            d_copy(par, dx, dy, q, (1 - dx, 1 - dy)).wait_send()

        each_side(x_side, y_side)
        each_corner(at_corner)

    def wait_halo(par, q):
        def x_side(side):
            for at in coming(q):
                x_copy(par, 1, side, at, side).wait_recv()
            x_copy(par, 0, side, q, 1 - side).wait_send()

        def y_side(side):
            for at in coming(q):
                y_copy(par, 1, side, at, side).wait_recv()
            y_copy(par, 0, side, q, 1 - side).wait_send()

        each_side(x_side, y_side)

    def lone_copies(side, arriving):
        land = side if arriving else 1 - side
        found = [
            (has_x[side], remote(near_x.at[side], raw_by.at[land], lone_send.at[0, side], lone_recv.at[0, land], at_x[side])),
            (has_y[side], remote(near_y.at[side], raw_bx.at[land], lone_send.at[1, side], lone_recv.at[1, land], at_y[side])),
        ]
        for dy in sides:
            other = dy if arriving else 1 - dy
            found.append((jnp.logical_and(has_x[side], has_y[dy]), remote(
                near_d.at[side, dy], raw_d.at[land, other], lone_send.at[2 + dy, side], lone_recv.at[2 + other, land],
                (at_x[side][0], at_y[dy][1]))))
        return found

    def raw_copies(q, arriving):
        cut = lanes(q)
        found = []
        for side in sides:
            land = side if arriving else 1 - side
            sources = (
                (has_x, at_x, 0, beta_ref.at[0, X - 1, :, cut], rim_x.at[:, cut]),
                (has_y, at_y, 1, rim_face.at[:, cut], rim_y.at[:, cut]),
                (has_x, at_x, 2, grad_ref.at[(X - 1) * side, :, cut], raw_x.at[0, land, :, cut]),
                (has_y, at_y, 3, grad_y.at[side, :, cut], raw_y.at[0, land, :, cut]),
                (has_x, at_x, 4, part_x.at[side, :, cut], raw_x.at[1, land, :, cut]),
                (has_y, at_y, 5, part_y.at[side, :, cut], raw_y.at[1, land, :, cut]),
            )
            for has, at, kind, source, landing in sources:
                if kind > 1 or side == (0 if arriving else 1):
                    found.append((has[side], remote(
                        source, landing, raw_send.at[kind, side, q], raw_recv.at[kind, land, q], at[side])))
        return found

    first = omega_of(STEPS - 1)

    def keep_faces(kind, value, x, g, cut):
        if g == 0:
            face_y[kind, 0, x : x + 1, cut] = value[:1, :]
        if g == groups - 1:
            face_y[kind, 1, x : x + 1, cut] = value[ROWS - 1 :, :]
        if kind == 0 and x in (0, X - 1):
            if g == 0:
                corner[0 if x == 0 else 1, 0, :, cut] = value[:1, :]
            if g == groups - 1:
                corner[0 if x == 0 else 1, 1, :, cut] = value[ROWS - 1 :, :]

    def prepare(x, g, q=None):
        r = slice(g * ROWS, (g + 1) * ROWS)
        start, stop = (0, Z) if q is None else (q * WIDE, (q + 1) * WIDE)
        cut = slice(start, stop)
        wide = slice(max(start - LANES, 0), stop)
        inner = slice(start - wide.start, stop - wide.start)
        z_at = z_ids[:, cut]
        up_x, up_y, up_z = beta_ref[0, x, r, cut], beta_ref[1, x, r, cut], beta_ref[2, x, r, wide]
        low_x = rim_x[r, cut] if x == 0 else beta_ref[0, x - 1, r, cut]
        row = rim_y[x : x + 1, cut] if g == 0 else beta_ref[1, x, g * ROWS - 1 : g * ROWS, cut]
        low_y = from_below(up_y, row)
        low_z = jnp.where(z_at == 0, 0.0, pltpu.roll(up_z, 1, 1)[:, inner])
        up_z = up_z[:, inner]
        inv = 1.0 / (up_x + low_x + up_y + low_y + up_z + low_z)
        up_z = jnp.where(z_at == Z - 1, 0.0, up_z)
        for index, value in enumerate((up_x, low_x, up_y, low_y, up_z, low_z)):
            value = value * inv
            coeff[index, x, r, cut] = value
            if index == 3 and g == 0:
                face_coeff[0, x : x + 1, cut] = value[:1, :]
            if index == 2 and g == groups - 1:
                face_coeff[1, x : x + 1, cut] = value[ROWS - 1 :, :]
        value = inv * grad_ref[x, r, cut]
        target[x, r, cut] = value
        state[1, x, r, cut] = first * value

    def prepare_halo_x(side, q):
        cut = slice(q * WIDE, (q + 1) * WIDE)
        for g in range(groups):
            r = slice(g * ROWS, (g + 1) * ROWS)
            shared = beta_ref[0, X - 1, r, cut] if side else rim_x[r, cut]
            total_of = raw_x[1, side, r, cut]
            if side:
                total_of += shared
            if g == 0:
                total_of += jnp.where(row_index(WIDE) == 0, raw_d[side, 0, 1, :, cut], 0.0)
            inv = 1.0 / total_of
            halo_x[1, 1, side, r, cut] = first * (inv * raw_x[0, side, r, cut])
            edge_x[side, r, cut] = shared * inv
            if g == 0:
                line_x[side, 0, :, cut] = raw_d[side, 0, 1, :, cut] * inv[:1, :]
            if g == groups - 1:
                line_x[side, 1, :, cut] = raw_by[side, :, cut] * inv[ROWS - 1 :, :]

    def prepare_halo_y(side, q):
        cut = slice(q * WIDE, (q + 1) * WIDE)
        shared = rim_face[:, cut] if side else rim_y[:, cut]
        total_of = raw_y[1, side, :, cut]
        if side:
            total_of += shared
        planes = lax.broadcasted_iota(jnp.int32, (X, WIDE), 0)
        total_of += jnp.where(planes == 0, raw_d[0, side, 0, :, cut], 0.0)
        inv = 1.0 / total_of
        halo_y[1, 1, side, :, cut] = first * (inv * raw_y[0, side, :, cut])
        edge_y[side, :, cut] = shared * inv
        line_y[side, 0, :, cut] = raw_d[0, side, 0, :, cut] * inv[:1, :]
        line_y[side, 1, :, cut] = raw_bx[side, :, cut] * inv[X - 1 :, :]

    def update_all(kind, omega, q, par=None):
        source = 1 - kind
        low, high = reach(kind, q)
        cut = slice(low, high)
        start, stop = max(low - LANES, 0), min(high + LANES, Z)
        inner = slice(low - start, high - start)
        rows = [slice(g * ROWS, (g + 1) * ROWS) for g in range(groups)]
        at_top, at_bottom = row_index(high - low) == ROWS - 1, row_index(high - low) == 0

        def plane(x):
            return [state[source, x, r, start:stop] for r in rows]

        before, here, after = None, plane(0), None
        for x in range(X):
            after = plane(x + 1) if x < X - 1 else None
            middle = [tile[:, inner] for tile in here]
            ups = [pltpu.roll(tile, ROWS - 1, 0) for tile in middle]
            downs = [pltpu.roll(tile, 1, 0) for tile in middle]
            edges = [0.0, 0.0] if par is None else [halo_y[par, 1, side, x : x + 1, cut] for side in sides]
            for g, r in enumerate(rows):
                s = middle[g]
                beside = target[x, r, cut] - s
                beside += coeff[2, x, r, cut] * jnp.where(at_top, ups[g + 1] if g < groups - 1 else edges[1], ups[g])
                beside += coeff[3, x, r, cut] * jnp.where(at_bottom, downs[g - 1] if g > 0 else edges[0], downs[g])
                beside += coeff[4, x, r, cut] * pltpu.roll(here[g], stop - start - 1, 1)[:, inner]
                beside += coeff[5, x, r, cut] * pltpu.roll(here[g], 1, 1)[:, inner]
                if x < X - 1:
                    beside += coeff[0, x, r, cut] * after[g][:, inner]
                elif par is not None:
                    beside += coeff[0, x, r, cut] * halo_x[par, 1, 1, r, cut]
                if x > 0:
                    beside += coeff[1, x, r, cut] * before[g]
                elif par is not None:
                    beside += coeff[1, x, r, cut] * halo_x[par, 1, 0, r, cut]
                value = s + omega * beside
                state[kind, x, r, cut] = value
                keep_faces(kind, value, x, g, cut)
            before, here = middle, after

    def complete_own(par, omega, q):
        cut = slice(q * WIDE, (q + 1) * WIDE)
        for side in sides:
            x = (X - 1) * side
            for g in range(groups):
                r = slice(g * ROWS, (g + 1) * ROWS)
                state[1, x, r, cut] += omega * (coeff[1 - side, x, r, cut] * halo_x[par, 0, side, r, cut])
        for side in sides:
            more = omega * (face_coeff[side, :, cut] * halo_y[par, 0, side, :, cut])
            row = (Y - 1) * side
            for x in range(X):
                state[1, x, row : row + 1, cut] += more[x : x + 1, :]

    def complete_halo(par, omega, q):
        cut = slice(*reach(1, q))
        for side in sides:
            x = (X - 1) * side
            for g in range(groups):
                r = slice(g * ROWS, (g + 1) * ROWS)
                halo_x[par, 1, side, r, cut] += omega * (edge_x[side, r, cut] * state[0, x, r, cut])
            for dy in sides:
                row = (Y - 1) * dy
                halo_x[par, 1, side, row : row + 1, cut] += omega * (
                    line_x[side, dy, :, cut] * halo_d[par, side, dy, :, cut])
        for side in sides:
            halo_y[par, 1, side, :, cut] += omega * (edge_y[side, :, cut] * face_y[0, side, :, cut])
            for dx in sides:
                x = (X - 1) * dx
                halo_y[par, 1, side, x : x + 1, cut] += omega * (
                    line_y[side, dx, :, cut] * halo_d[par, dx, side, :, cut])

    for side in sides:
        for has, copy in lone_copies(side, False):
            @pl.when(has)
            def _():
                copy.start()
    for q in range(chunks):
        for has, copy in raw_copies(q, False):
            @pl.when(has)
            def _():
                copy.start()

    for name in ("owner", "slot"):
        loads[name].wait()

    owner = owner_ref[...]
    peer_ids = lax.broadcasted_iota(jnp.int32, (peers, tiles), 0)
    named = (owner == peer_ids).astype(jnp.float32)
    down = lax.broadcasted_iota(jnp.int32, (tiles, tiles), 0)
    across = lax.broadcasted_iota(jnp.int32, (tiles, tiles), 1)
    earlier = (down < across).astype(jnp.bfloat16)
    counts = jnp.dot(named.astype(jnp.bfloat16), earlier, preferred_element_type=jnp.float32)
    position = jnp.sum(counts * named, axis=0, keepdims=True)
    spot = owner.astype(jnp.float32) * CAP + position
    spots = lax.broadcasted_iota(jnp.int32, (peers * CAP, tiles), 0).astype(jnp.float32)
    place[...] = (spot == spots).astype(jnp.float32).astype(jnp.bfloat16)
    spread = lax.broadcasted_iota(jnp.int32, (LANES, tiles), 0).astype(jnp.float32)
    spread = (spread == position).astype(jnp.float32)
    slot_rows = lax.dot_general(
        named * slot_ref[...].astype(jnp.float32), spread, (((1,), (1,)), ((), ())),
        preferred_element_type=jnp.float32, precision=EXACT,
    )
    send_slots[...] = slot_rows.reshape(peers, 1, LANES)

    @pl.loop(1, peers, unroll=True)
    def _(step):
        slot_copy(step).start()

    recv_slots[me] = send_slots[me]
    for x in range(1, X):
        for g in range(1, groups):
            prepare(x, g)

    for name in ("rows", "mask", "heights"):
        loads[name].wait()

    @pl.loop(0, tiles // UNROLL)
    def _(part):
        for lane in range(UNROLL):
            t = part * UNROLL + lane
            row = rows_ref[t]
            line = lax.div(row, blocks)
            x = lax.div(line, Y)
            spots_ref[t] = (x * blocks + row - line * blocks) * Y + line - x * Y

    slope = 0.5 * (heights_ref[2] - heights_ref[0])
    bend = heights_ref[2] - 2.0 * heights_ref[1] + heights_ref[0]
    denom = 1.0 + slope * slope
    factor = 1.0 / (denom * jnp.sqrt(denom))
    skew = -3.0 * slope * bend * factor / denom
    scales[0] = factor - 0.5 * skew
    scales[1] = -2.0 * factor
    scales[2] = factor + 0.5 * skew

    for side in sides:
        for has, copy in lone_copies(side, True):
            @pl.when(has)
            def _():
                copy.wait_recv()

    def begin(q):
        for has, copy in raw_copies(q, True):
            @pl.when(has)
            def _():
                copy.wait_recv()
        for g in range(1, groups):
            prepare(0, g, q)
        for x in range(X):
            prepare(x, 0, q)
        for side in sides:
            @pl.when(has_x[side])
            def _():
                prepare_halo_x(side, q)

            @pl.when(has_y[side])
            def _():
                prepare_halo_y(side, q)

    def second(q):
        update_all(1, omega_of(STEPS - 1 - 2 % STEPS), q)
        start_sends(0, 1, q)

    begin(0)
    for q in range(chunks):
        if q + 1 < chunks:
            begin(q + 1)
        update_all(0, omega_of(STEPS - 1 - 1 % STEPS), q, 1)
        start_sends(0, 0, q)
        second(q)

    def round_body(number, carry):
        par = number % 2
        more = number < rounds - 1
        omega = omega_at(2 * number + 2)
        omega_even = omega_at(2 * number + 3)
        omega_odd = omega_at(2 * number + 4)

        def own(q):
            wait_own(par, q)
            complete_own(par, omega, q)

        def odd(q):
            @pl.when(more)
            def _():
                update_all(1, omega_odd, q)
                start_sends(1 - par, 1, q)

        own(0)
        for q in range(chunks):
            if q + 1 < chunks:
                own(q + 1)
            wait_halo(par, q)
            for at in coming(q):
                complete_halo(par, omega, at)
            update_all(0, omega_even, q, par)

            @pl.when(more)
            def _():
                start_sends(1 - par, 0, q)

            odd(q)
        return carry

    lax.fori_loop(0, rounds, round_body, 0)
    keep = pltpu.make_async_copy(state.at[0], out_ref, load_sem.at[7])
    keep.start()
    for x in range(X):
        for b in range(blocks):
            start = (x * blocks + b) * Y
            flat[start : start + Y, :] = state[0, x, :, b * LANES : (b + 1) * LANES]

    @pl.loop(0, tiles // UNROLL)
    def _(part):
        for lane in range(UNROLL):
            t = part * UNROLL + lane
            picked[pl.ds(t, 1), :] = flat[pl.ds(spots_ref[t], 1), :]

    jumps = picked[...] * mask_ref[...].astype(jnp.float32)
    send_rows[...] = picked_sum(place[...], jumps).reshape(peers, CAP, LANES)

    @pl.loop(1, peers, unroll=True)
    def _(step):
        row_copy(step).start()

    recv_rows[me] = send_rows[me]
    for side in sides:
        for has, copy in lone_copies(side, False):
            @pl.when(has)
            def _():
                copy.wait_send()
    for q in range(chunks):
        for has, copy in raw_copies(q, False):
            @pl.when(has)
            def _():
                copy.wait_send()

    @pl.loop(1, peers, unroll=True)
    def _(step):
        peer, place_of = peer_at(step)
        pltpu.make_async_remote_copy(
            send_slots.at[peer], recv_slots.at[peer], slot_send.at[peer], slot_recv.at[peer],
            device_id=place_of, device_id_type=MESH).wait()

    own = lax.broadcasted_iota(jnp.int32, (peers, CAP, LANES), 1)
    lane_ids = lax.broadcasted_iota(jnp.int32, (peers, CAP, LANES), 2)
    got = jnp.broadcast_to(recv_slots[...], (peers, CAP, LANES))
    slot_of = jnp.sum(jnp.where(own == lane_ids, got, 0.0), axis=2, keepdims=True)
    slot_of = slot_of.reshape(peers * CAP, 1)
    slot_ids = lax.broadcasted_iota(jnp.int32, (peers * CAP, slots), 1).astype(jnp.float32)
    chosen[...] = (slot_of == slot_ids).astype(jnp.float32).T.astype(jnp.bfloat16)

    @pl.loop(1, peers, unroll=True)
    def _(step):
        peer, place_of = peer_at(step)
        pltpu.make_async_remote_copy(
            send_rows.at[peer], recv_rows.at[peer], row_send.at[peer], row_recv.at[peer],
            device_id=place_of, device_id_type=MESH).wait()

    table = picked_sum(chosen[...], recv_rows[...].reshape(peers * CAP, LANES))
    for index in range(3):
        back_ref[index] = table * scales[index]
    keep.wait()


def hand_over(first_held, second_held, first_out, second_out, sem):
    stores = []
    for held, landing in ((first_held, first_out), (second_held, second_out)):
        for index in range(held.shape[0]):
            stores.append(pltpu.make_async_copy(held.at[index], landing.at[index], sem.at[len(stores)]))
    for store in stores:
        store.start()
    for store in stores:
        store.wait()


def shards(grad_pressure, beta, tile_rows, tile_owner, tile_slot, face_mask, heights):
    n_x, n_y = lax.axis_size("gx"), lax.axis_size("gy")
    peers = n_x * n_y
    X, Y, Z = grad_pressure.shape
    chunks = Z // WIDE
    tiles = tile_rows.shape[0]
    f32 = jnp.float32
    vmem = pl.BlockSpec(memory_space=pltpu.VMEM)
    hbm = pl.BlockSpec(memory_space=pltpu.HBM)
    dma = pltpu.SemaphoreType.DMA
    results = pl.pallas_call(
        functools.partial(kernel, n_x, n_y),
        out_shape=(pltpu.VMEM((X, Y, Z), f32), pltpu.VMEM(heights.shape, f32)),
        in_specs=[hbm] * 7,
        out_specs=(vmem, vmem),
        scratch_shapes=[
            pltpu.VMEM((X, Y, Z), f32),
            pltpu.VMEM(beta.shape, f32),
            pltpu.SMEM((tiles,), jnp.int32),
            pltpu.VMEM((1, tiles), jnp.int32),
            pltpu.VMEM((1, tiles), jnp.int32),
            pltpu.VMEM(face_mask.shape, jnp.int32),
            pltpu.VMEM(heights.shape, f32),
            dma((8,)),
            pltpu.VMEM((6, X, Y, Z), f32),
            pltpu.VMEM((X, Y, Z), f32),
            pltpu.VMEM((2, X, Y, Z), f32),
            pltpu.VMEM((2, 2, X, Z), f32),
            pltpu.VMEM((2, 2, 1, Z), f32),
            pltpu.VMEM((2, 2, 2, Y, Z), f32),
            pltpu.VMEM((2, 2, 2, X, Z), f32),
            pltpu.VMEM((2, 2, 2, 1, Z), f32),
            pltpu.VMEM((Y, Z), f32),
            pltpu.VMEM((X, Z), f32),
            pltpu.VMEM((X, Z), f32),
            pltpu.VMEM((2, X, Z), f32),
            pltpu.VMEM((2, Y, Z), f32),
            pltpu.VMEM((2, X, Z), f32),
            pltpu.VMEM((2, 2, 1, Z), f32),
            pltpu.VMEM((2, 2, 1, Z), f32),
            pltpu.VMEM((2, Y, Z), f32),
            pltpu.VMEM((2, X, Z), f32),
            pltpu.VMEM((2, X, Z), f32),
            pltpu.VMEM((2, 1, Z), f32),
            pltpu.VMEM((2, 1, Z), f32),
            pltpu.VMEM((2, 2, 2, 1, Z), f32),
            pltpu.VMEM((2, 2, Y, Z), f32),
            pltpu.VMEM((2, 2, X, Z), f32),
            pltpu.VMEM((2, 1, Z), f32),
            pltpu.VMEM((2, 1, Z), f32),
            pltpu.VMEM((2, 2, 2, 1, Z), f32),
            pltpu.VMEM((X * Y * Z // LANES, LANES), f32),
            pltpu.VMEM((tiles, LANES), f32),
            pltpu.SMEM((tiles,), jnp.int32),
            pltpu.VMEM((heights.shape[1], peers * CAP), jnp.bfloat16),
            pltpu.VMEM(heights.shape, f32),
            pltpu.VMEM((peers * CAP, tiles), jnp.bfloat16),
            pltpu.VMEM((peers, CAP, LANES), f32),
            pltpu.VMEM((peers, CAP, LANES), f32),
            pltpu.VMEM((peers, 1, LANES), f32),
            pltpu.VMEM((peers, 1, LANES), f32),
            dma((2, 2, chunks)),
            dma((2, 2, 2, chunks)),
            dma((2, 2, chunks)),
            dma((2, 2, 2, chunks)),
            dma((2, 2, chunks)),
            dma((2, 2, 2, chunks)),
            dma((6, 2, chunks)),
            dma((6, 2, chunks)),
            dma((4, 2)),
            dma((4, 2)),
            dma((peers,)),
            dma((peers,)),
            dma((peers,)),
            dma((peers,)),
        ],
        compiler_params=pltpu.CompilerParams(
            collective_id=0, has_side_effects=True, vmem_limit_bytes=60 * 1024 * 1024
        ),
    )(grad_pressure, beta, tile_rows, tile_owner.reshape(1, -1), tile_slot.reshape(1, -1), face_mask, heights)
    parts = sum(result.shape[0] for result in results)
    return pl.pallas_call(
        hand_over,
        out_shape=tuple(jax.ShapeDtypeStruct(result.shape, f32) for result in results),
        in_specs=[vmem] * 2,
        out_specs=(hbm, hbm),
        scratch_shapes=[dma((parts,))],
    )(*[pltpu.with_memory_space_constraint(result, pltpu.VMEM) for result in results])


def solution(mesh):
    in_specs = (
        P("gx", "gy", None),
        P(None, "gx", "gy", None),
        P(("gx", "gy")),
        P(("gx", "gy"), None),
        P(("gx", "gy")),
        P(("gx", "gy"), None),
        P(None, ("gx", "gy"), None),
    )
    out_specs = (P("gx", "gy", None), P(None, ("gx", "gy"), None))
    return jax.shard_map(shards, mesh=mesh, in_specs=in_specs, out_specs=out_specs, check_vma=False)
```
